512 devices in a mesh: section: 16 (over z, y_hi), dp: 32 (over x, y_lo, core).
Axes of the slice: x: 4, y: 8 (y_hi: 2, y_lo: 4; y = y_hi * 4 + y_lo), z: 8, core: 2. Of those that a mesh axis runs over, the one named last changes fastest.
Arguments:
- tokens: bfloat16 [8192, 4096], P('dp'), may hold values from -48 to 48
- orig_weight: bfloat16 [16384, 4096], P(('section', 'dp')), may hold values from -6 to 6
- keep_flags: int32 [64], replicated, may hold values from 0 to 1, as said below
Outputs:
- corrected: bfloat16 [16384, 4096], P(('section', 'dp'))
The draws below stay inside these ranges and needn't reach their ends.
Inputs may be any that keep to these rules, and one draw needn't show every extreme that they name: `keep_flags`: exactly 12 of the 64 flags are 1.
All inputs are finite; a program needn't handle non-finite values.
Results may differ from the reference program's by a relative error of at most 0.003.
Values may be sent and summed in bfloat16 or wider, within the bound.
A program may use at most 64 MiB of HBM per device.

```python
import jax
import jax.numpy as jnp
from jax import lax

K = 4096
NBLK = 64
KEEP_BLK = 12
KEEP = 768
TOK_DEV = 256
ROWS = 16384
TOKENS = 8192


def block_ranks(key):
    return jax.random.permutation(jax.random.fold_in(key, 21), NBLK)


def draw_tokens(key, part):
    key_noise = jax.random.fold_in(key, 11)
    key_latent = jax.random.fold_in(key, 12)
    key_map = jax.random.fold_in(key, 13)
    key_amp = jax.random.fold_in(key, 14)
    key_block = jax.random.fold_in(key, 15)
    key_cols = jax.random.fold_in(key, 16)
    key_sign = jax.random.fold_in(key, 19)
    blocks = TOKENS // TOK_DEV
    factors = max(KEEP // 4, 8)
    noise = jnp.clip(jax.random.normal(key_noise, (TOKENS, K), jnp.float32), -5.0, 5.0)
    latent = jnp.clip(jax.random.normal(key_latent, (TOKENS, factors), jnp.float32), -5.0, 5.0)
    factor_map = jax.random.randint(key_map, (K,), 0, factors)
    signs = (2 * jax.random.randint(key_sign, (K,), 0, 2) - 1).astype(jnp.float32)
    amplitude = 5.9 * signs * jnp.exp(jax.random.uniform(key_amp, (K,), jnp.float32, -0.5, 0.5))
    shared = jnp.take(latent, factor_map, axis=1) * amplitude[None, :]
    mixed = noise + shared
    kept_block = (block_ranks(key) < KEEP_BLK).astype(jnp.float32)
    boost = jnp.repeat(1.0 + 0.41421356 * kept_block, 64)
    col_scale = jnp.exp(jax.random.uniform(key_cols, (K,), jnp.float32, -0.3, 0.3)) * boost
    block_scale = jnp.exp(jax.random.uniform(key_block, (blocks, NBLK), jnp.float32, 0.0, 1.0))
    levels = 1.0 + 2.0 * jnp.arange(blocks, dtype=jnp.float32) / max(blocks - 1, 1)
    region_scale = jnp.repeat(block_scale * levels[:, None], 64, axis=1)
    token_scale = jnp.repeat(region_scale, TOK_DEV, axis=0)
    result = 0.1 * mixed * token_scale * col_scale[None, :]
    result = jnp.clip(result, -48.0, 48.0)
    return result.astype(jnp.bfloat16)


def draw_keep_flags(key, part):
    return (block_ranks(key) < KEEP_BLK).astype(jnp.int32)


def steps_of(own_key, shape, split, smallest, largest):
    loudness, own = 1.0, jax.random.fold_in(own_key, 6)
    for position, shards_of in split:
        draws = jnp.exp(jax.random.uniform(jax.random.fold_in(own, position), (shards_of,), jnp.float32, smallest / len(split), largest / len(split)))
        loudness = loudness * jnp.repeat(draws, shape[position] // shards_of).reshape([-1 if axis == position else 1 for axis in range(len(shape))])
    return loudness


def gaussian(rng, extent, deviation, most, pieces=(), held_as=jnp.bfloat16):
    factor_of = steps_of(rng, extent, pieces, -0.22, 0.18) if pieces else 1.0
    array = jax.random.normal(rng, extent, jnp.float32) * deviation * factor_of
    return jnp.minimum(jnp.maximum(array, -most), most).astype(held_as)


def setup_inputs(seed: int = 0) -> dict:
    splits = jax.random.split(jax.random.key(seed), 4)
    return {
        "tokens": draw_tokens(jax.random.fold_in(splits[3], 71), 0),
        "orig_weight": gaussian(splits[1], (ROWS, K), 1.0, 6.0, ((0, 512),)),
        "keep_flags": draw_keep_flags(jax.random.fold_in(splits[3], 71), 0),
    }


def reference(tokens, orig_weight, keep_flags):
    highest = lax.Precision.HIGHEST
    blocks = jnp.nonzero(keep_flags, size=KEEP_BLK)[0].astype(jnp.int32)
    kept_index = (blocks[:, None] * 64 + jnp.arange(64, dtype=jnp.int32)[None, :]).reshape(-1).astype(jnp.int32)
    kept_tokens = jnp.take(tokens, kept_index, axis=1).astype(jnp.float32)
    wide_tokens = tokens.astype(jnp.float32)
    gramian = jnp.dot(kept_tokens.T, kept_tokens, precision=highest)
    damping = 0.01 * jnp.sum(wide_tokens * wide_tokens) / K
    cross = jnp.dot(kept_tokens.T, wide_tokens, precision=highest)
    right_side = jnp.dot(cross, orig_weight.astype(jnp.float32).T, precision=highest)
    system = gramian + damping * jnp.eye(KEEP, dtype=jnp.float32)
    factor = jnp.linalg.cholesky(system)
    solution = jax.scipy.linalg.cho_solve((factor, True), right_side)
    corrected = jnp.zeros((ROWS, K), jnp.float32).at[:, kept_index].set(solution.T)
    return corrected.astype(jnp.bfloat16)
```

```python
import functools

import jax
import jax.numpy as jnp
from jax import lax
from jax.experimental import pallas as pl
from jax.experimental.pallas import tpu as pltpu
from jax.sharding import PartitionSpec as P

HIGHEST = lax.Precision.HIGHEST
F32 = jnp.float32
BF16 = jnp.bfloat16
MESH = pl.DeviceIdType.MESH

KEEP_BLK = 12
KEEP = 768
TILE = 128
PANEL = 8
NBLOCK = KEEP // TILE
UNITS = NBLOCK * (NBLOCK + 1) // 2
WIDE = KEEP + TILE
CHUNK = 256


def _lower_block(t):
    row = jnp.int32(0)
    for i in range(1, NBLOCK):
        row = row + (t >= i * (i + 1) // 2).astype(jnp.int32)
    return row, t - row * (row + 1) // 2


def _half_swap(v):
    return pltpu.roll(v, 64, 1)


def prepare_kernel(flags, tokens, part, kept, kept_tokens, gram):
    section = lax.axis_index("section")

    def note(b, count):
        kept[count] = b
        return count + flags[b]

    lax.fori_loop(0, 64, note, jnp.int32(0))
    low = lax.broadcasted_iota(jnp.int32, (256, TILE), 1) < 64
    for i in range(NBLOCK):
        first, second = kept[2 * i], kept[2 * i + 1]
        a = tokens[:, pl.ds(pl.multiple_of((first // 2) * TILE, TILE), TILE)].astype(F32)
        b = tokens[:, pl.ds(pl.multiple_of((second // 2) * TILE, TILE), TILE)].astype(F32)
        a = jnp.where(first % 2 == 1, _half_swap(a), a)
        b = jnp.where(second % 2 == 0, _half_swap(b), b)
        kept_tokens[:, i * TILE : (i + 1) * TILE] = jnp.where(low, a, b).astype(BF16)
    chunk = tokens[:, pl.ds(pl.multiple_of(section * CHUNK, CHUNK), CHUNK)]
    over_tokens = (((0,), (0,)), ((), ()))
    part[:, 0:KEEP] = lax.dot_general(
        chunk, kept_tokens[...], over_tokens, preferred_element_type=F32
    )
    gram[...] = lax.dot_general(
        kept_tokens[...], kept_tokens[...], over_tokens, preferred_element_type=F32
    )
    for u in range(UNITS):
        unit = section * UNITS + u
        row, col = _lower_block(unit // 16)
        start = row * TILE + (unit % 16) * 8
        part[8 * u : 8 * u + 8, KEEP:WIDE] = gram[
            pl.ds(pl.multiple_of(start, 8), 8), pl.ds(pl.multiple_of(col * TILE, TILE), TILE)
        ]
    wide = chunk.astype(F32)
    squares = wide * wide
    squares = squares[:, :TILE] + squares[:, TILE:]
    total = squares[0:8]
    for g in range(1, 32):
        total = total + squares[8 * g : 8 * g + 8]
    part[8 * UNITS : 8 * UNITS + 8, KEEP:WIDE] = total
    part[8 * UNITS + 8 : 256, KEEP:WIDE] = jnp.zeros((256 - 8 * UNITS - 8, TILE), F32)


def tile_inverse(rows):
    lane = lax.broadcasted_iota(jnp.int32, (8, TILE), 1)
    sub = lax.broadcasted_iota(jnp.int32, (8, TILE), 0)
    panels = TILE // PANEL

    def over_lanes(v, c):
        return jnp.broadcast_to(v[:, c : c + 1], (8, TILE))

    def over_rows(v, q):
        return jnp.broadcast_to(v[q : q + 1, :], (8, TILE))

    for j in range(panels):
        base = j * PANEL
        columns = [over_lanes(rows[j], base + c) for c in range(PANEL)]
        inside = (lane >= base) & (lane < base + PANEL)
        r = jnp.where(inside, (lane - base == sub).astype(F32), rows[j])
        for q in range(PANEL):
            inv = 1.0 / over_rows(columns[q], q)
            pivot = sub == q
            m = jnp.where(pivot, 0.0, columns[q] * inv)
            scale = jnp.where(pivot, inv, 1.0)
            r = r * scale - m * over_rows(r, q)
            for c in range(q + 1, PANEL):
                columns[c] = columns[c] * scale - m * over_rows(columns[c], q)
        spread = [over_rows(r, c) for c in range(PANEL)]
        after = []
        for g in range(panels):
            if g == j:
                after.append(r)
                continue
            acc = jnp.where(inside, 0.0, rows[g])
            for c in range(PANEL):
                acc = acc - over_lanes(rows[g], base + c) * spread[c]
            after.append(acc)
        rows = after
    return rows


def eliminate(k, m, d):
    off = pl.multiple_of(k * TILE, TILE)
    rows = [m[pl.ds(pl.multiple_of(off + 8 * g, 8), 8), pl.ds(off, TILE)] for g in range(TILE // 8)]
    rows = tile_inverse(rows)
    for g in range(TILE // 8):
        d[8 * g : 8 * g + 8, :] = rows[g]
    col = lax.broadcasted_iota(jnp.int32, (TILE, KEEP), 1) - off
    row = lax.broadcasted_iota(jnp.int32, (TILE, KEEP), 0)
    inside = (col >= 0) & (col < TILE)
    r = jnp.where(inside, (col == row).astype(F32), m[pl.ds(off, TILE), :])
    r = jnp.dot(d[...], r, precision=HIGHEST, preferred_element_type=F32)
    for b in range(KEEP // 256):
        at = slice(256 * b, 256 * b + 256)
        c = m[at, pl.ds(off, TILE)]
        col = lax.broadcasted_iota(jnp.int32, (256, KEEP), 1) - off
        rest = jnp.where((col >= 0) & (col < TILE), 0.0, m[at, :])
        m[at, :] = rest - jnp.dot(c, r, precision=HIGHEST, preferred_element_type=F32)
    m[pl.ds(off, TILE), :] = r


def solve_kernel(
    part, weight, out,
    from_core, from_x, from_y, sums, shares, g_all, c_all, w_all, right, from_z, m, d, send, recv,
):
    section, dp = lax.axis_index("section"), lax.axis_index("dp")
    z, far = section // 2, section % 2
    x, y, core = dp // 8, (dp // 2) % 4, dp % 2

    def peer(axis, o):
        if axis == "z":
            return (lax.rem(z + o, 8) * 2 + far, dp)
        if axis == "far":
            return (z * 2 + 1 - far, dp)
        if axis == "x":
            return (section, lax.rem(x + o, 4) * 8 + y * 2 + core)
        if axis == "y":
            return (section, x * 8 + lax.rem(y + o, 4) * 2 + core)
        return (section, x * 8 + y * 2 + 1 - core)

    sizes = {"z": 8, "far": 2, "x": 4, "y": 4, "core": 2}
    barrier = pltpu.get_barrier_semaphore()
    greeted = 0
    for axis, n in sizes.items():
        for o in range(1, n):
            pl.semaphore_signal(barrier, inc=1, device_id=peer(axis, o), device_id_type=MESH)
            greeted += 1
    pl.semaphore_wait(barrier, greeted)

    slots = [0]

    def exchange(axis, source, target, landed):
        first = slots[0]
        n = sizes[axis]
        slots[0] += n - 1

        def copy(o, dst):
            at = first + o - 1
            return pltpu.make_async_remote_copy(
                src_ref=source(o), dst_ref=dst, send_sem=send.at[at], recv_sem=recv.at[at],
                device_id=peer(axis, o), device_id_type=MESH,
            )

        def start():
            for o in range(1, n):
                copy(o, target(o)).start()

        def wait():
            for o in range(1, n):
                copy(o, landed(o)).wait_send()
            for o in range(1, n):
                copy(o, landed(o)).wait_recv()

        return start, wait

    def at8(v, n=8):
        return pl.multiple_of(v, n)

    w_start, w_wait = exchange(
        "z",
        lambda o: weight.at[:, pl.ds(at8(lax.rem(z + o, 8) * 512, 512), 512)],
        lambda o: w_all.at[pl.ds(at8(z * 32, 32), 32), :],
        lambda o: w_all.at[pl.ds(at8(lax.rem(z + 8 - o, 8) * 32, 32), 32), :],
    )
    w_start()

    lanes = {"g": slice(KEEP, WIDE), "c": slice(0, KEEP)}
    stage = {}
    for name in ("g", "c"):
        cut = lanes[name]
        stage[name, "core"] = exchange(
            "core",
            lambda o, cut=cut: part.at[pl.ds(at8((1 - core) * 128, 128), 128), cut],
            lambda o, cut=cut: from_core.at[:, cut],
            lambda o, cut=cut: from_core.at[:, cut],
        )
        stage[name, "x"] = exchange(
            "x",
            lambda o, cut=cut: sums.at[pl.ds(at8(lax.rem(x + o, 4) * 32, 32), 32), cut],
            lambda o, cut=cut: from_x.at[o - 1, :, cut],
            lambda o, cut=cut: from_x.at[o - 1, :, cut],
        )
        stage[name, "y"] = exchange(
            "y",
            lambda o, cut=cut: shares.at[pl.ds(at8(lax.rem(y + o, 4) * 8), 8), cut],
            lambda o, cut=cut: from_y.at[o - 1, :, cut],
            lambda o, cut=cut: from_y.at[o - 1, :, cut],
        )

    def add_core(cut):
        sums[:, cut] = part[pl.ds(at8(core * 128, 128), 128), cut] + from_core[:, cut]

    def add_x(cut):
        own = sums[pl.ds(at8(x * 32, 32), 32), cut]
        shares[:, cut] = own + from_x[0, :, cut] + from_x[1, :, cut] + from_x[2, :, cut]

    def add_y(cut):
        own = shares[pl.ds(at8(y * 8), 8), cut]
        return own + from_y[0, :, cut] + from_y[1, :, cut] + from_y[2, :, cut]

    base = at8(core * 128 + x * 32 + y * 8)
    g_cut, c_cut = lanes["g"], lanes["c"]
    stage["g", "core"][0]()
    stage["c", "core"][0]()
    stage["g", "core"][1]()
    add_core(g_cut)
    stage["g", "x"][0]()
    stage["c", "core"][1]()
    add_core(c_cut)
    stage["c", "x"][0]()
    stage["g", "x"][1]()
    add_x(g_cut)
    stage["g", "y"][0]()
    stage["g", "y"][1]()
    g_all[z, far, pl.ds(base, 8), :] = add_y(g_cut)

    gz = exchange(
        "z",
        lambda o: g_all.at[z, far, pl.ds(base, 8), :],
        lambda o: g_all.at[z, far, pl.ds(base, 8), :],
        lambda o: g_all.at[lax.rem(z + 8 - o, 8), far, pl.ds(base, 8), :],
    )
    gfar = exchange(
        "far",
        lambda o: g_all.at[:, far, pl.ds(base, 8), :],
        lambda o: g_all.at[:, far, pl.ds(base, 8), :],
        lambda o: g_all.at[:, 1 - far, pl.ds(base, 8), :],
    )

    def row8(o):
        return at8(core * 128 + x * 32 + lax.rem(y + 4 - o, 4) * 8)

    def row32(o):
        return at8(core * 128 + lax.rem(x + 4 - o, 4) * 32, 32)

    gy = exchange(
        "y",
        lambda o: g_all.at[:, :, pl.ds(base, 8), :],
        lambda o: g_all.at[:, :, pl.ds(base, 8), :],
        lambda o: g_all.at[:, :, pl.ds(row8(o), 8), :],
    )
    gx = exchange(
        "x",
        lambda o: g_all.at[:, :, pl.ds(row32(0), 32), :],
        lambda o: g_all.at[:, :, pl.ds(row32(0), 32), :],
        lambda o: g_all.at[:, :, pl.ds(row32(o), 32), :],
    )
    gcore = exchange(
        "core",
        lambda o: g_all.at[:, :, pl.ds(at8(core * 128, 128), 128), :],
        lambda o: g_all.at[:, :, pl.ds(at8(core * 128, 128), 128), :],
        lambda o: g_all.at[:, :, pl.ds(at8((1 - core) * 128, 128), 128), :],
    )
    cfar = exchange(
        "far",
        lambda o: c_all.at[far, pl.ds(base, 8), :],
        lambda o: c_all.at[far, pl.ds(base, 8), :],
        lambda o: c_all.at[1 - far, pl.ds(base, 8), :],
    )
    cy = exchange(
        "y",
        lambda o: c_all.at[:, pl.ds(base, 8), :],
        lambda o: c_all.at[:, pl.ds(base, 8), :],
        lambda o: c_all.at[:, pl.ds(row8(o), 8), :],
    )
    cx = exchange(
        "x",
        lambda o: c_all.at[:, pl.ds(row32(0), 32), :],
        lambda o: c_all.at[:, pl.ds(row32(0), 32), :],
        lambda o: c_all.at[:, pl.ds(row32(o), 32), :],
    )
    ccore = exchange(
        "core",
        lambda o: c_all.at[:, pl.ds(at8(core * 128, 128), 128), :],
        lambda o: c_all.at[:, pl.ds(at8(core * 128, 128), 128), :],
        lambda o: c_all.at[:, pl.ds(at8((1 - core) * 128, 128), 128), :],
    )
    rz = exchange(
        "z",
        lambda o: right.at[pl.ds(at8(lax.rem(z + o, 8) * 32, 32), 32), :],
        lambda o: from_z.at[o - 1],
        lambda o: from_z.at[o - 1],
    )

    gz[0]()
    stage["c", "x"][1]()
    add_x(c_cut)
    stage["c", "y"][0]()
    gz[1]()
    gfar[0]()
    stage["c", "y"][1]()
    c_all[far, pl.ds(base, 8), :] = add_y(c_cut)
    cfar[0]()
    gfar[1]()
    gy[0]()
    cfar[1]()
    gy[1]()
    gx[0]()
    gx[1]()
    gcore[0]()
    cy[0]()
    w_all[pl.ds(at8(z * 32, 32), 32), :] = weight[:, pl.ds(at8(z * 512, 512), 512)]
    gcore[1]()

    total = jnp.zeros((8, TILE), F32)
    for s in range(16):
        total = total + g_all[s // 2, s % 2, 8 * UNITS : 8 * UNITS + 8, :]
    total = jnp.sum(jnp.sum(total, axis=0, keepdims=True), axis=1, keepdims=True)
    damping = 0.01 * total / 4096.0
    for t in range(UNITS):
        i = max(n for n in range(NBLOCK) if n * (n + 1) // 2 <= t)
        j = t - i * (i + 1) // 2
        for e in range(16):
            s, u = divmod(t * 16 + e, UNITS)
            m[i * TILE + 8 * e : i * TILE + 8 * e + 8, j * TILE : (j + 1) * TILE] = g_all[
                s // 2, s % 2, 8 * u : 8 * u + 8, :
            ]
        block = m[i * TILE : (i + 1) * TILE, j * TILE : (j + 1) * TILE]
        if i == j:
            eye = lax.broadcasted_iota(jnp.int32, (TILE, TILE), 0) == lax.broadcasted_iota(
                jnp.int32, (TILE, TILE), 1
            )
            m[i * TILE : (i + 1) * TILE, j * TILE : (j + 1) * TILE] = block + jnp.where(
                eye, damping, 0.0
            )
        else:
            m[j * TILE : (j + 1) * TILE, i * TILE : (i + 1) * TILE] = block.T

    def right_side():
        for b in range(2):
            c = c_all[b]
            high = c.astype(BF16)
            c = c - high.astype(F32)
            middle = c.astype(BF16)
            low = (c - middle.astype(F32)).astype(BF16)
            w = w_all[:, b * 256 : (b + 1) * 256]
            term = jnp.dot(w, high, preferred_element_type=F32)
            term += jnp.dot(w, middle, preferred_element_type=F32)
            term += jnp.dot(w, low, preferred_element_type=F32)
            if b == 0:
                right[...] = term
            else:
                right[...] += term

    @pl.loop(0, NBLOCK)
    def _(k):
        @pl.when(k == 0)
        def _():
            cy[1]()
            cx[0]()

        @pl.when(k == 1)
        def _():
            cx[1]()
            ccore[0]()

        @pl.when(k == 2)
        def _():
            ccore[1]()
            w_wait()
            right_side()
            rz[0]()

        eliminate(k, m, d)

    rz[1]()
    own = right[pl.ds(at8(z * 32, 32), 32), :]
    for o in range(7):
        own = own + from_z[o]
    out[...] = jnp.dot(own, m[...], precision=HIGHEST, preferred_element_type=F32)


def spread_kernel(flags, solved, out):
    low = lax.broadcasted_iota(jnp.int32, (32, TILE), 1) < 64
    rank = jnp.int32(0)
    for g in range(32):
        sides = []
        for side in range(2):
            flag = flags[2 * g + side]
            at = jnp.minimum(rank, KEEP_BLK - 1)
            v = solved[:, pl.ds(pl.multiple_of((at // 2) * TILE, TILE), TILE)]
            v = jnp.where(at % 2 == side, v, _half_swap(v))
            sides.append(jnp.where(flag == 1, v, 0.0))
            rank = rank + flag
        out[:, g * TILE : (g + 1) * TILE] = jnp.where(low, sides[0], sides[1]).astype(BF16)


def on_device(tokens, orig_weight, keep_flags):
    vmem = pl.BlockSpec(memory_space=pltpu.VMEM)
    smem = pl.BlockSpec(memory_space=pltpu.SMEM)
    part = pl.pallas_call(
        prepare_kernel,
        out_shape=jax.ShapeDtypeStruct((256, WIDE), F32),
        in_specs=[smem, vmem],
        out_specs=vmem,
        scratch_shapes=[
            pltpu.SMEM((16,), jnp.int32),
            pltpu.VMEM((256, KEEP), BF16),
            pltpu.VMEM((KEEP, KEEP), F32),
        ],
        name="prepare",
    )(keep_flags, tokens)
    solved = pl.pallas_call(
        solve_kernel,
        out_shape=jax.ShapeDtypeStruct((32, KEEP), F32),
        in_specs=[vmem, vmem],
        out_specs=vmem,
        scratch_shapes=[
            pltpu.VMEM((128, WIDE), F32),
            pltpu.VMEM((3, 32, WIDE), F32),
            pltpu.VMEM((3, 8, WIDE), F32),
            pltpu.VMEM((128, WIDE), F32),
            pltpu.VMEM((32, WIDE), F32),
            pltpu.VMEM((8, 2, 256, TILE), F32),
            pltpu.VMEM((2, 256, KEEP), F32),
            pltpu.VMEM((256, 512), BF16),
            pltpu.VMEM((256, KEEP), F32),
            pltpu.VMEM((7, 32, KEEP), F32),
            pltpu.VMEM((KEEP, KEEP), F32),
            pltpu.VMEM((TILE, TILE), F32),
            pltpu.SemaphoreType.DMA((64,)),
            pltpu.SemaphoreType.DMA((64,)),
        ],
        compiler_params=pltpu.CompilerParams(collective_id=0, has_side_effects=True),
        name="solve",
    )(part, orig_weight)
    return pl.pallas_call(
        spread_kernel,
        out_shape=jax.ShapeDtypeStruct((32, orig_weight.shape[1]), BF16),
        in_specs=[smem, vmem],
        out_specs=vmem,
        name="spread",
    )(keep_flags, solved)


def solution(mesh):
    in_specs = (P("dp", None), P(("section", "dp"), None), P())
    out_specs = P(("section", "dp"), None)
    return jax.shard_map(
        on_device, mesh=mesh, in_specs=in_specs, out_specs=out_specs, check_vma=False
    )
```

```python
import functools

import jax
import jax.numpy as jnp
from jax import lax
from jax.experimental import pallas as pl
from jax.experimental.pallas import tpu as pltpu
from jax.sharding import PartitionSpec as P

HIGHEST = lax.Precision.HIGHEST
F32 = jnp.float32
BF16 = jnp.bfloat16
MESH = pl.DeviceIdType.MESH

KEEP_BLK = 12
KEEP = 768
TILE = 128
PANEL = 8
NBLOCK = KEEP // TILE
FIRST = NBLOCK
LATER = NBLOCK * (NBLOCK - 1) // 2
WIDE = KEEP + TILE
CHUNK = 256


def _lower_block(t):
    row = jnp.int32(0)
    for i in range(1, NBLOCK - 1):
        row = row + (t >= i * (i + 1) // 2).astype(jnp.int32)
    return row, t - row * (row + 1) // 2


def _half_swap(v):
    return pltpu.roll(v, 64, 1)


def prepare_kernel(flags, tokens, part, kept, kept_tokens, gram):
    section = lax.axis_index("section")

    def note(b, count):
        kept[count] = b
        return count + flags[b]

    lax.fori_loop(0, 64, note, jnp.int32(0))
    low = lax.broadcasted_iota(jnp.int32, (256, TILE), 1) < 64
    for i in range(NBLOCK):
        first, second = kept[2 * i], kept[2 * i + 1]
        a = tokens[:, pl.ds(pl.multiple_of((first // 2) * TILE, TILE), TILE)].astype(F32)
        b = tokens[:, pl.ds(pl.multiple_of((second // 2) * TILE, TILE), TILE)].astype(F32)
        a = jnp.where(first % 2 == 1, _half_swap(a), a)
        b = jnp.where(second % 2 == 0, _half_swap(b), b)
        kept_tokens[:, i * TILE : (i + 1) * TILE] = jnp.where(low, a, b).astype(BF16)
    chunk = tokens[:, pl.ds(pl.multiple_of(section * CHUNK, CHUNK), CHUNK)]
    over_tokens = (((0,), (0,)), ((), ()))
    part[:, 0:KEEP] = lax.dot_general(
        chunk, kept_tokens[...], over_tokens, preferred_element_type=F32
    )
    gram[...] = lax.dot_general(
        kept_tokens[...], kept_tokens[...], over_tokens, preferred_element_type=F32
    )
    part[:, KEEP:WIDE] = jnp.zeros((256, TILE), F32)

    def put(at, unit, row, col):
        start = row * TILE + (unit % 16) * 8
        part[at : at + 8, KEEP:WIDE] = gram[
            pl.ds(pl.multiple_of(start, 8), 8), pl.ds(pl.multiple_of(col * TILE, TILE), TILE)
        ]

    for u in range(FIRST):
        unit = section * FIRST + u
        put(32 * u, unit, unit // 16, 0)
    for u in range(LATER):
        unit = section * LATER + u
        row, col = _lower_block(unit // 16)
        put(32 * (u % 8) + 8 * (1 + u // 8), unit, row + 1, col + 1)
    wide = chunk.astype(F32)
    squares = wide * wide
    squares = squares[:, :TILE] + squares[:, TILE:]
    total = squares[0:8]
    for g in range(1, 32):
        total = total + squares[8 * g : 8 * g + 8]
    part[32 * FIRST : 32 * FIRST + 8, KEEP:WIDE] = total


def tile_factors(rows, n, t, scratch):
    lane = lax.broadcasted_iota(jnp.int32, (8, TILE), 1)
    sub = lax.broadcasted_iota(jnp.int32, (8, TILE), 0)
    panels = TILE // PANEL
    rows = list(rows)

    def over_lanes(v, c):
        column = jnp.sum(jnp.where(lane == c, v, 0.0), axis=1, keepdims=True)
        return jnp.broadcast_to(column, (8, TILE))

    def over_rows(v, q):
        return jnp.broadcast_to(v[q : q + 1, :], (8, TILE))

    for j in range(panels):
        base = j * PANEL
        for c in range(PANEL):
            scratch[8 * c : 8 * c + 8, :] = over_lanes(rows[j], base + c)
        columns = [scratch[8 * c : 8 * c + 8, :] for c in range(PANEL)]
        inside = (lane >= base) & (lane < base + PANEL)
        r = jnp.where(inside, (lane - base == sub).astype(F32), rows[j])
        n[base : base + 8, :] = jnp.where(lane < base + PANEL, r, 0.0)
        for q in range(PANEL):
            inv = 1.0 / over_rows(columns[q], q)
            pivot = sub == q
            m = jnp.where(pivot, 0.0, columns[q] * inv)
            scale = jnp.where(pivot, inv, 1.0)
            r = r * scale - m * over_rows(r, q)
            for c in range(q + 1, PANEL):
                columns[c] = columns[c] * scale - m * over_rows(columns[c], q)
        t[base : base + 8, :] = jnp.where(lane < base + PANEL, r, 0.0)
        spread = [over_rows(r, c) for c in range(PANEL)]
        for g in range(j + 1, panels):
            acc = jnp.where(inside, 0.0, rows[g])
            for c in range(PANEL):
                acc = acc - over_lanes(rows[g], base + c) * spread[c]
            rows[g] = acc


def pieces(v):
    high = v.astype(BF16)
    v = v - high.astype(F32)
    middle = v.astype(BF16)
    return high, middle, (v - middle.astype(F32)).astype(BF16)


def put_left(ref, rows, v):
    high, middle, low = pieces(v)
    for i, p in enumerate((high, high, middle, middle, high, low)):
        ref[rows, i * TILE : (i + 1) * TILE] = p


def put_right(ref, v):
    high, middle, low = pieces(v)
    for i, p in enumerate((high, middle, high, middle, low, high)):
        ref[i * TILE : (i + 1) * TILE, :] = p


def eliminate(k, m, lower, n, t, scratch, left, right, arrive):
    off = pl.multiple_of(k * TILE, TILE)
    rows = [m[pl.ds(pl.multiple_of(off + 8 * g, 8), 8), pl.ds(off, TILE)] for g in range(TILE // 8)]
    tile_factors(rows, n, t, scratch)
    arrive()
    d = lax.dot_general(
        n[...], t[...], (((0,), (0,)), ((), ())), precision=HIGHEST, preferred_element_type=F32
    )
    col = lax.broadcasted_iota(jnp.int32, (TILE, KEEP), 1) - off
    row = lax.broadcasted_iota(jnp.int32, (TILE, KEEP), 0)
    inside = (col >= 0) & (col < TILE)
    r = jnp.where(inside, (col == row).astype(F32), m[pl.ds(off, TILE), :])
    lower[pl.ds(off, TILE), :] = jnp.where(col < TILE, r, 0.0)
    put_left(left, slice(0, TILE), d)
    put_right(right, r)
    r = jnp.dot(left[0:TILE, :], right[...], preferred_element_type=F32)
    m[pl.ds(off, TILE), :] = jnp.where(col < TILE, r, 0.0)
    put_right(right, r)
    for kk in range(NBLOCK - 1):

        @pl.when(k == kk)
        def _():
            start = kk * TILE
            stop = start + TILE
            put_left(left, slice(stop, KEEP), m[stop:KEEP, start:stop])
            p = jnp.dot(left[stop:KEEP, :], right[...], preferred_element_type=F32)
            if kk:
                m[stop:KEEP, 0:start] = m[stop:KEEP, 0:start] - p[:, 0:start]
            m[stop:KEEP, start:stop] = -p[:, start:stop]
            m[stop:KEEP, stop:KEEP] = m[stop:KEEP, stop:KEEP] - p[:, stop:KEEP]


def solve_kernel(
    part, weight, out,
    from_core, from_x, from_y, sums, shares, g_all, c_all, w_all, right, from_z,
    m, lower, n_tile, t_tile, scratch, left_pieces, right_pieces, send, recv,
):
    section, dp = lax.axis_index("section"), lax.axis_index("dp")
    z, far = section // 2, section % 2
    x, y, core = dp // 8, (dp // 2) % 4, dp % 2
    slot = lax.rem(y + 3, 4)

    def peer(axis, o):
        if axis == "z":
            return (lax.rem(z + o, 8) * 2 + far, dp)
        if axis == "far":
            return (z * 2 + 1 - far, dp)
        if axis == "x":
            return (section, lax.rem(x + o, 4) * 8 + y * 2 + core)
        if axis == "y":
            return (section, x * 8 + lax.rem(y + o, 4) * 2 + core)
        return (section, x * 8 + y * 2 + 1 - core)

    sizes = {"z": 8, "far": 2, "x": 4, "y": 4, "core": 2}
    barrier = pltpu.get_barrier_semaphore()
    greeted = 0
    for axis, n in sizes.items():
        for o in range(1, n):
            pl.semaphore_signal(barrier, inc=1, device_id=peer(axis, o), device_id_type=MESH)
            greeted += 1
    pl.semaphore_wait(barrier, greeted)

    slots = [0]

    def exchange(axis, source, target, landed):
        first = slots[0]
        n = sizes[axis]
        slots[0] += n - 1

        def copy(o, dst):
            at = first + o - 1
            return pltpu.make_async_remote_copy(
                src_ref=source(o), dst_ref=dst, send_sem=send.at[at], recv_sem=recv.at[at],
                device_id=peer(axis, o), device_id_type=MESH,
            )

        def start():
            for o in range(1, n):
                copy(o, target(o)).start()

        def wait():
            for o in range(1, n):
                copy(o, landed(o)).wait_send()
            for o in range(1, n):
                copy(o, landed(o)).wait_recv()

        return start, wait

    def at8(v, n=8):
        return pl.multiple_of(v, n)

    w_start, w_wait = exchange(
        "z",
        lambda o: weight.at[:, pl.ds(at8(lax.rem(z + o, 8) * 512, 512), 512)],
        lambda o: w_all.at[pl.ds(at8(z * 32, 32), 32), :],
        lambda o: w_all.at[pl.ds(at8(lax.rem(z + 8 - o, 8) * 32, 32), 32), :],
    )
    w_start()

    lanes = {"g": slice(KEEP, WIDE), "c": slice(0, KEEP)}
    stage = {}
    for name in ("g", "c"):
        cut = lanes[name]
        stage[name, "core"] = exchange(
            "core",
            lambda o, cut=cut: part.at[pl.ds(at8((1 - core) * 128, 128), 128), cut],
            lambda o, cut=cut: from_core.at[:, cut],
            lambda o, cut=cut: from_core.at[:, cut],
        )
        stage[name, "x"] = exchange(
            "x",
            lambda o, cut=cut: sums.at[pl.ds(at8(lax.rem(x + o, 4) * 32, 32), 32), cut],
            lambda o, cut=cut: from_x.at[o - 1, :, cut],
            lambda o, cut=cut: from_x.at[o - 1, :, cut],
        )
        stage[name, "y"] = exchange(
            "y",
            lambda o, cut=cut: shares.at[pl.ds(at8(lax.rem(slot + o, 4) * 8), 8), cut],
            lambda o, cut=cut: from_y.at[o - 1, :, cut],
            lambda o, cut=cut: from_y.at[o - 1, :, cut],
        )

    def add_core(cut):
        sums[:, cut] = part[pl.ds(at8(core * 128, 128), 128), cut] + from_core[:, cut]

    def add_x(cut):
        own = sums[pl.ds(at8(x * 32, 32), 32), cut]
        shares[:, cut] = own + from_x[0, :, cut] + from_x[1, :, cut] + from_x[2, :, cut]

    def add_y(cut):
        own = shares[pl.ds(at8(slot * 8), 8), cut]
        return own + from_y[0, :, cut] + from_y[1, :, cut] + from_y[2, :, cut]

    base = at8(core * 128 + x * 32 + slot * 8)
    g_cut, c_cut = lanes["g"], lanes["c"]
    stage["g", "core"][0]()
    stage["c", "core"][0]()
    stage["g", "core"][1]()
    add_core(g_cut)
    stage["g", "x"][0]()
    stage["c", "core"][1]()
    add_core(c_cut)
    stage["c", "x"][0]()
    stage["g", "x"][1]()
    add_x(g_cut)
    stage["g", "y"][0]()
    stage["g", "y"][1]()
    own8 = pl.ds(at8(slot * 8), 8)
    g_all[z, far, core, x, own8, :] = add_y(g_cut)

    gz = exchange(
        "z",
        lambda o: g_all.at[z, far, core, x, own8, :],
        lambda o: g_all.at[z, far, core, x, own8, :],
        lambda o: g_all.at[lax.rem(z + 8 - o, 8), far, core, x, own8, :],
    )
    gfar = exchange(
        "far",
        lambda o: g_all.at[:, far, core, x, own8, :],
        lambda o: g_all.at[:, far, core, x, own8, :],
        lambda o: g_all.at[:, 1 - far, core, x, own8, :],
    )

    def row8(o):
        return at8(core * 128 + x * 32 + lax.rem(slot + 4 - o, 4) * 8)

    def row32(o):
        return at8(core * 128 + lax.rem(x + 4 - o, 4) * 32, 32)

    y_slots = slots[0]
    slots[0] += 3

    def gy_copy(o):
        rows = pl.ds(at8(lax.rem(slot + 4 - o, 4) * 8), 8)
        return pltpu.make_async_remote_copy(
            src_ref=g_all.at[:, :, core, x, own8, :],
            dst_ref=g_all.at[:, :, core, x, rows, :],
            send_sem=send.at[y_slots + o - 1], recv_sem=recv.at[y_slots + o - 1],
            device_id=peer("y", o), device_id_type=MESH,
        )

    def gy_start():
        @pl.when(slot < 3)
        def _():
            for o in range(1, 4):
                pltpu.make_async_remote_copy(
                    src_ref=g_all.at[:, :, core, x, own8, :],
                    dst_ref=g_all.at[:, :, core, x, own8, :],
                    send_sem=send.at[y_slots + o - 1], recv_sem=recv.at[y_slots + o - 1],
                    device_id=peer("y", o), device_id_type=MESH,
                ).start()

    def gy_sent():
        @pl.when(slot < 3)
        def _():
            for o in range(1, 4):
                gy_copy(o).wait_send()

    def gy_wait(first):
        for o in range(1, 4):
            source = lax.rem(slot + 4 - o, 4)

            @pl.when((source == 0) if first else ((source == 1) | (source == 2)))
            def _():
                gy_copy(o).wait_recv()

    def gather_rest(rows):
        along_x = exchange(
            "x",
            lambda o: g_all.at[:, :, core, x, rows, :],
            lambda o: g_all.at[:, :, core, x, rows, :],
            lambda o: g_all.at[:, :, core, lax.rem(x + 4 - o, 4), rows, :],
        )
        along_core = exchange(
            "core",
            lambda o: g_all.at[:, :, core, :, rows, :],
            lambda o: g_all.at[:, :, core, :, rows, :],
            lambda o: g_all.at[:, :, 1 - core, :, rows, :],
        )
        return along_x, along_core

    first_x, first_core = gather_rest(slice(0, 8))
    later_x, later_core = gather_rest(slice(8, 24))
    cfar = exchange(
        "far",
        lambda o: c_all.at[far, pl.ds(base, 8), :],
        lambda o: c_all.at[far, pl.ds(base, 8), :],
        lambda o: c_all.at[1 - far, pl.ds(base, 8), :],
    )
    cy = exchange(
        "y",
        lambda o: c_all.at[:, pl.ds(base, 8), :],
        lambda o: c_all.at[:, pl.ds(base, 8), :],
        lambda o: c_all.at[:, pl.ds(row8(o), 8), :],
    )
    cx = exchange(
        "x",
        lambda o: c_all.at[:, pl.ds(row32(0), 32), :],
        lambda o: c_all.at[:, pl.ds(row32(0), 32), :],
        lambda o: c_all.at[:, pl.ds(row32(o), 32), :],
    )
    ccore = exchange(
        "core",
        lambda o: c_all.at[:, pl.ds(at8(core * 128, 128), 128), :],
        lambda o: c_all.at[:, pl.ds(at8(core * 128, 128), 128), :],
        lambda o: c_all.at[:, pl.ds(at8((1 - core) * 128, 128), 128), :],
    )
    rz = exchange(
        "z",
        lambda o: right.at[pl.ds(at8(lax.rem(z + o, 8) * 32, 32), 32), :],
        lambda o: from_z.at[o - 1],
        lambda o: from_z.at[o - 1],
    )

    gz[0]()
    stage["c", "x"][1]()
    add_x(c_cut)
    stage["c", "y"][0]()
    gz[1]()
    gfar[0]()
    stage["c", "y"][1]()
    c_all[far, pl.ds(base, 8), :] = add_y(c_cut)
    cfar[0]()
    gfar[1]()
    gy_start()
    cfar[1]()
    cy[0]()
    gy_wait(True)
    first_x[0]()
    gy_wait(False)
    later_x[0]()
    cy[1]()
    cx[0]()
    w_all[pl.ds(at8(z * 32, 32), 32), :] = weight[:, pl.ds(at8(z * 512, 512), 512)]
    first_x[1]()
    first_core[0]()
    gy_sent()
    first_core[1]()

    total = jnp.zeros((8, TILE), F32)
    for s in range(16):
        total = total + g_all[s // 2, s % 2, FIRST // 4, FIRST % 4, 0:8, :]
    total = jnp.sum(jnp.sum(total, axis=0, keepdims=True), axis=1, keepdims=True)
    damping = 0.01 * total / 4096.0

    def place(i, j, unit_at):
        rows, cols = slice(i * TILE, (i + 1) * TILE), slice(j * TILE, (j + 1) * TILE)
        for e in range(16):
            m[i * TILE + 8 * e : i * TILE + 8 * e + 8, cols] = unit_at(e)
        block = m[rows, cols]
        if i == j:
            eye = lax.broadcasted_iota(jnp.int32, (TILE, TILE), 0) == lax.broadcasted_iota(
                jnp.int32, (TILE, TILE), 1
            )
            m[rows, cols] = block + jnp.where(eye, damping, 0.0)
        else:
            m[cols, rows] = block.T

    for i in range(NBLOCK):

        def first_unit(e, i=i):
            s, u = divmod(i * 16 + e, FIRST)
            return g_all[s // 2, s % 2, u // 4, u % 4, 0:8, :]

        place(i, 0, first_unit)

    def later_blocks():
        later_x[1]()
        later_core[0]()
        later_core[1]()
        block = 0
        for i in range(1, NBLOCK):
            for j in range(1, i + 1):

                def later_unit(e, block=block):
                    s, u = divmod(block * 16 + e, LATER)
                    q = u % 8
                    at = 8 * (1 + u // 8)
                    return g_all[s // 2, s % 2, q // 4, q % 4, at : at + 8, :]

                place(i, j, later_unit)
                block += 1

    def right_side():
        for b in range(2):
            c = c_all[b]
            high = c.astype(BF16)
            c = c - high.astype(F32)
            middle = c.astype(BF16)
            low = (c - middle.astype(F32)).astype(BF16)
            w = w_all[:, b * 256 : (b + 1) * 256]
            term = jnp.dot(w, high, preferred_element_type=F32)
            term += jnp.dot(w, middle, preferred_element_type=F32)
            term += jnp.dot(w, low, preferred_element_type=F32)
            if b == 0:
                right[...] = term
            else:
                right[...] += term

    @pl.loop(0, NBLOCK)
    def _(k):
        @pl.when(k == 1)
        def _():
            cx[1]()
            ccore[0]()

        @pl.when(k == 2)
        def _():
            ccore[1]()
            w_wait()
            right_side()
            rz[0]()

        def arrive():
            pl.when(k == 0)(later_blocks)

        eliminate(
            k, m, lower, n_tile, t_tile, scratch, left_pieces, right_pieces, arrive
        )

    rz[1]()
    own = right[pl.ds(at8(z * 32, 32), 32), :]
    for o in range(7):
        own = own + from_z[o]
    own = lax.dot_general(
        own, lower[...], (((1,), (1,)), ((), ())), precision=HIGHEST, preferred_element_type=F32
    )
    out[...] = jnp.dot(own, m[...], precision=HIGHEST, preferred_element_type=F32)


def spread_kernel(flags, solved, out):
    low = lax.broadcasted_iota(jnp.int32, (32, TILE), 1) < 64
    rank = jnp.int32(0)
    for g in range(32):
        sides = []
        for side in range(2):
            flag = flags[2 * g + side]
            at = jnp.minimum(rank, KEEP_BLK - 1)
            v = solved[:, pl.ds(pl.multiple_of((at // 2) * TILE, TILE), TILE)]
            v = jnp.where(at % 2 == side, v, _half_swap(v))
            sides.append(jnp.where(flag == 1, v, 0.0))
            rank = rank + flag
        out[:, g * TILE : (g + 1) * TILE] = jnp.where(low, sides[0], sides[1]).astype(BF16)


def on_device(tokens, orig_weight, keep_flags):
    vmem = pl.BlockSpec(memory_space=pltpu.VMEM)
    smem = pl.BlockSpec(memory_space=pltpu.SMEM)
    part = pl.pallas_call(
        prepare_kernel,
        out_shape=jax.ShapeDtypeStruct((256, WIDE), F32),
        in_specs=[smem, vmem],
        out_specs=vmem,
        scratch_shapes=[
            pltpu.SMEM((16,), jnp.int32),
            pltpu.VMEM((256, KEEP), BF16),
            pltpu.VMEM((KEEP, KEEP), F32),
        ],
        name="prepare",
    )(keep_flags, tokens)
    solved = pl.pallas_call(
        solve_kernel,
        out_shape=jax.ShapeDtypeStruct((32, KEEP), F32),
        in_specs=[vmem, vmem],
        out_specs=vmem,
        scratch_shapes=[
            pltpu.VMEM((128, WIDE), F32),
            pltpu.VMEM((3, 32, WIDE), F32),
            pltpu.VMEM((3, 8, WIDE), F32),
            pltpu.VMEM((128, WIDE), F32),
            pltpu.VMEM((32, WIDE), F32),
            pltpu.VMEM((8, 2, 2, 4, 32, TILE), F32),
            pltpu.VMEM((2, 256, KEEP), F32),
            pltpu.VMEM((256, 512), BF16),
            pltpu.VMEM((256, KEEP), F32),
            pltpu.VMEM((7, 32, KEEP), F32),
            pltpu.VMEM((KEEP, KEEP), F32),
            pltpu.VMEM((KEEP, KEEP), F32),
            pltpu.VMEM((TILE, TILE), F32),
            pltpu.VMEM((TILE, TILE), F32),
            pltpu.VMEM((8 * PANEL, TILE), F32),
            pltpu.VMEM((KEEP, KEEP), BF16),
            pltpu.VMEM((KEEP, KEEP), BF16),
            pltpu.SemaphoreType.DMA((64,)),
            pltpu.SemaphoreType.DMA((64,)),
        ],
        compiler_params=pltpu.CompilerParams(collective_id=0, has_side_effects=True),
        name="solve",
    )(part, orig_weight)
    return pl.pallas_call(
        spread_kernel,
        out_shape=jax.ShapeDtypeStruct((32, orig_weight.shape[1]), BF16),
        in_specs=[smem, vmem],
        out_specs=vmem,
        name="spread",
    )(keep_flags, solved)


def solution(mesh):
    in_specs = (P("dp", None), P(("section", "dp"), None), P())
    out_specs = P(("section", "dp"), None)
    return jax.shard_map(
        on_device, mesh=mesh, in_specs=in_specs, out_specs=out_specs, check_vma=False
    )
```

```python
import functools

import jax
import jax.numpy as jnp
from jax import lax
from jax.experimental import pallas as pl
from jax.experimental.pallas import tpu as pltpu
from jax.sharding import PartitionSpec as P

HIGHEST = lax.Precision.HIGHEST
F32 = jnp.float32
BF16 = jnp.bfloat16
MESH = pl.DeviceIdType.MESH

KEEP_BLK = 12
KEEP = 768
TILE = 128
PANEL = 8
NBLOCK = KEEP // TILE
FIRST = NBLOCK
LATER = NBLOCK * (NBLOCK - 1) // 2
WIDE = KEEP + TILE
CHUNK = 256


def _lower_block(t):
    row = jnp.int32(0)
    for i in range(1, NBLOCK - 1):
        row = row + (t >= i * (i + 1) // 2).astype(jnp.int32)
    return row, t - row * (row + 1) // 2


def _half_swap(v):
    return pltpu.roll(v, 64, 1)


def prepare_kernel(flags, tokens, part, kept, kept_tokens, gram):
    section = lax.axis_index("section")

    def note(b, count):
        kept[count] = b
        return count + flags[b]

    lax.fori_loop(0, 64, note, jnp.int32(0))
    low = lax.broadcasted_iota(jnp.int32, (256, TILE), 1) < 64
    for i in range(NBLOCK):
        first, second = kept[2 * i], kept[2 * i + 1]
        a = tokens[:, pl.ds(pl.multiple_of((first // 2) * TILE, TILE), TILE)].astype(F32)
        b = tokens[:, pl.ds(pl.multiple_of((second // 2) * TILE, TILE), TILE)].astype(F32)
        a = jnp.where(first % 2 == 1, _half_swap(a), a)
        b = jnp.where(second % 2 == 0, _half_swap(b), b)
        kept_tokens[:, i * TILE : (i + 1) * TILE] = jnp.where(low, a, b).astype(BF16)
    chunk = tokens[:, pl.ds(pl.multiple_of(section * CHUNK, CHUNK), CHUNK)]
    over_tokens = (((0,), (0,)), ((), ()))
    part[:, 0:KEEP] = lax.dot_general(
        chunk, kept_tokens[...], over_tokens, preferred_element_type=F32
    )
    gram[...] = lax.dot_general(
        kept_tokens[...], kept_tokens[...], over_tokens, preferred_element_type=F32
    )
    part[:, KEEP:WIDE] = jnp.zeros((256, TILE), F32)

    def put(at, unit, row, col):
        start = row * TILE + (unit % 16) * 8
        part[at : at + 8, KEEP:WIDE] = gram[
            pl.ds(pl.multiple_of(start, 8), 8), pl.ds(pl.multiple_of(col * TILE, TILE), TILE)
        ]

    for u in range(FIRST):
        unit = section * FIRST + u
        put(32 * u, unit, unit // 16, 0)
    for u in range(LATER):
        unit = section * LATER + u
        row, col = _lower_block(unit // 16)
        put(32 * (u % 8) + 8 * (1 + u // 8), unit, row + 1, col + 1)
    wide = chunk.astype(F32)
    squares = wide * wide
    squares = squares[:, :TILE] + squares[:, TILE:]
    total = squares[0:8]
    for g in range(1, 32):
        total = total + squares[8 * g : 8 * g + 8]
    part[32 * FIRST : 32 * FIRST + 8, KEEP:WIDE] = total


def tile_factors(rows, n, t, scratch):
    lane = lax.broadcasted_iota(jnp.int32, (8, TILE), 1)
    sub = lax.broadcasted_iota(jnp.int32, (8, TILE), 0)
    panels = TILE // PANEL
    rows = list(rows)

    def over_lanes(v, c):
        column = jnp.sum(jnp.where(lane == c, v, 0.0), axis=1, keepdims=True)
        return jnp.broadcast_to(column, (8, TILE))

    def over_rows(v, q):
        return jnp.broadcast_to(v[q : q + 1, :], (8, TILE))

    for j in range(panels):
        base = j * PANEL
        for c in range(PANEL):
            scratch[8 * c : 8 * c + 8, :] = over_lanes(rows[j], base + c)
        columns = [scratch[8 * c : 8 * c + 8, :] for c in range(PANEL)]
        inside = (lane >= base) & (lane < base + PANEL)
        r = jnp.where(inside, (lane - base == sub).astype(F32), rows[j])
        n[base : base + 8, :] = jnp.where(lane < base + PANEL, r, 0.0)
        for q in range(PANEL):
            inv = 1.0 / over_rows(columns[q], q)
            pivot = sub == q
            m = jnp.where(pivot, 0.0, columns[q] * inv)
            scale = jnp.where(pivot, inv, 1.0)
            r = r * scale - m * over_rows(r, q)
            for c in range(q + 1, PANEL):
                columns[c] = columns[c] * scale - m * over_rows(columns[c], q)
        t[base : base + 8, :] = jnp.where(lane < base + PANEL, r, 0.0)
        spread = [over_rows(r, c) for c in range(PANEL)]
        for g in range(j + 1, panels):
            acc = jnp.where(inside, 0.0, rows[g])
            for c in range(PANEL):
                acc = acc - over_lanes(rows[g], base + c) * spread[c]
            rows[g] = acc


def pieces(v):
    high = v.astype(BF16)
    v = v - high.astype(F32)
    middle = v.astype(BF16)
    return high, middle, (v - middle.astype(F32)).astype(BF16)


def put_left(ref, rows, v):
    high, middle, low = pieces(v)
    for i, p in enumerate((high, high, middle, middle, high, low)):
        ref[rows, i * TILE : (i + 1) * TILE] = p


def put_right(ref, v):
    high, middle, low = pieces(v)
    for i, p in enumerate((high, middle, high, middle, low, high)):
        ref[i * TILE : (i + 1) * TILE, :] = p


def eliminate(k, m, lower, n, t, scratch, left, right, arrive):
    off = pl.multiple_of(k * TILE, TILE)
    rows = [m[pl.ds(pl.multiple_of(off + 8 * g, 8), 8), pl.ds(off, TILE)] for g in range(TILE // 8)]
    tile_factors(rows, n, t, scratch)
    arrive()
    d = lax.dot_general(
        n[...], t[...], (((0,), (0,)), ((), ())), precision=HIGHEST, preferred_element_type=F32
    )
    col = lax.broadcasted_iota(jnp.int32, (TILE, KEEP), 1) - off
    row = lax.broadcasted_iota(jnp.int32, (TILE, KEEP), 0)
    inside = (col >= 0) & (col < TILE)
    r = jnp.where(inside, (col == row).astype(F32), m[pl.ds(off, TILE), :])
    lower[pl.ds(off, TILE), :] = jnp.where(col < TILE, r, 0.0)
    put_left(left, slice(0, TILE), d)
    put_right(right, r)
    r = jnp.dot(left[0:TILE, :], right[...], preferred_element_type=F32)
    m[pl.ds(off, TILE), :] = jnp.where(col < TILE, r, 0.0)
    put_right(right, r)
    for kk in range(NBLOCK - 1):

        @pl.when(k == kk)
        def _():
            start = kk * TILE
            stop = start + TILE
            put_left(left, slice(stop, KEEP), m[stop:KEEP, start:stop])
            p = jnp.dot(left[stop:KEEP, :], right[...], preferred_element_type=F32)
            if kk:
                m[stop:KEEP, 0:start] = m[stop:KEEP, 0:start] - p[:, 0:start]
            m[stop:KEEP, start:stop] = -p[:, start:stop]
            m[stop:KEEP, stop:KEEP] = m[stop:KEEP, stop:KEEP] - p[:, stop:KEEP]


def solve_kernel(
    part, weight, out,
    from_core, from_x, from_y, sums, shares, g_all, c_all, w_all, right, from_z,
    m, lower, n_tile, t_tile, scratch, left_pieces, right_pieces, send, recv,
):
    section, dp = lax.axis_index("section"), lax.axis_index("dp")
    z, far = section // 2, section % 2
    x, y, core = dp // 8, (dp // 2) % 4, dp % 2
    slot = lax.rem(y + 3, 4)

    def peer(axis, o):
        if axis == "z":
            return (lax.rem(z + o, 8) * 2 + far, dp)
        if axis == "ring":
            at = lax.rem(far * 4 + y + o, 8)
            return (z * 2 + at // 4, x * 8 + lax.rem(at, 4) * 2 + core)
        if axis == "x":
            return (section, lax.rem(x + o, 4) * 8 + y * 2 + core)
        if axis == "y":
            return (section, x * 8 + lax.rem(y + o, 4) * 2 + core)
        return (section, x * 8 + y * 2 + 1 - core)

    sizes = {"z": 8, "ring": 8, "x": 4, "y": 4, "core": 2}
    barrier = pltpu.get_barrier_semaphore()
    greeted = 0
    for axis in ("z", "ring", "x", "core"):
        for o in range(1, sizes[axis]):
            pl.semaphore_signal(barrier, inc=1, device_id=peer(axis, o), device_id_type=MESH)
            greeted += 1
    pl.semaphore_wait(barrier, greeted)

    slots = [0]

    def exchange(axis, source, target, landed):
        first = slots[0]
        n = sizes[axis]
        slots[0] += n - 1

        def copy(o, dst):
            at = first + o - 1
            return pltpu.make_async_remote_copy(
                src_ref=source(o), dst_ref=dst, send_sem=send.at[at], recv_sem=recv.at[at],
                device_id=peer(axis, o), device_id_type=MESH,
            )

        def start():
            for o in range(1, n):
                copy(o, target(o)).start()

        def wait():
            for o in range(1, n):
                copy(o, landed(o)).wait_send()
            for o in range(1, n):
                copy(o, landed(o)).wait_recv()

        return start, wait

    def at8(v, n=8):
        return pl.multiple_of(v, n)

    w_start, w_wait = exchange(
        "z",
        lambda o: weight.at[:, pl.ds(at8(lax.rem(z + o, 8) * 512, 512), 512)],
        lambda o: w_all.at[pl.ds(at8(z * 32, 32), 32), :],
        lambda o: w_all.at[pl.ds(at8(lax.rem(z + 8 - o, 8) * 32, 32), 32), :],
    )
    w_start()

    halves = (0, 1)
    lanes = {"g": slice(KEEP, WIDE), 0: slice(0, KEEP // 2), 1: slice(KEEP // 2, KEEP)}
    stage = {}
    for name in ("g", 0, 1):
        cut = lanes[name]
        stage[name, "core"] = exchange(
            "core",
            lambda o, cut=cut: part.at[pl.ds(at8((1 - core) * 128, 128), 128), cut],
            lambda o, cut=cut: from_core.at[:, cut],
            lambda o, cut=cut: from_core.at[:, cut],
        )
        stage[name, "x"] = exchange(
            "x",
            lambda o, cut=cut: sums.at[pl.ds(at8(lax.rem(x + o, 4) * 32, 32), 32), cut],
            lambda o, cut=cut: from_x.at[o - 1, :, cut],
            lambda o, cut=cut: from_x.at[o - 1, :, cut],
        )
        stage[name, "y"] = exchange(
            "y",
            lambda o, cut=cut: shares.at[pl.ds(at8(lax.rem(slot + o, 4) * 8), 8), cut],
            lambda o, cut=cut: from_y.at[o - 1, :, cut],
            lambda o, cut=cut: from_y.at[o - 1, :, cut],
        )

    def add_core(cut):
        sums[:, cut] = part[pl.ds(at8(core * 128, 128), 128), cut] + from_core[:, cut]

    def add_x(cut):
        own = sums[pl.ds(at8(x * 32, 32), 32), cut]
        shares[:, cut] = own + from_x[0, :, cut] + from_x[1, :, cut] + from_x[2, :, cut]

    def add_y(cut):
        own = shares[pl.ds(at8(slot * 8), 8), cut]
        return own + from_y[0, :, cut] + from_y[1, :, cut] + from_y[2, :, cut]

    base = at8(core * 128 + x * 32 + slot * 8)
    g_cut = lanes["g"]
    stage["g", "core"][0]()
    for h in halves:
        stage[h, "core"][0]()

    def c_to_x(h):
        stage[h, "core"][1]()
        add_core(lanes[h])
        stage[h, "x"][0]()

    def c_to_y(h):
        stage[h, "x"][1]()
        add_x(lanes[h])
        stage[h, "y"][0]()

    stage["g", "core"][1]()
    add_core(g_cut)
    stage["g", "x"][0]()
    c_to_x(0)
    stage["g", "x"][1]()
    add_x(g_cut)
    stage["g", "y"][0]()
    c_to_x(1)
    stage["g", "y"][1]()
    own8 = pl.ds(at8(slot * 8), 8)
    g_all[z, far, core, x, own8, :] = add_y(g_cut)

    gz = exchange(
        "z",
        lambda o: g_all.at[z, far, core, x, own8, :],
        lambda o: g_all.at[z, far, core, x, own8, :],
        lambda o: g_all.at[lax.rem(z + 8 - o, 8), far, core, x, own8, :],
    )
    def ring_source(o):
        at = lax.rem(far * 4 + y + 8 - o, 8)
        return at // 4, lax.rem(at + 3, 4)

    def row32(o):
        return at8(core * 128 + lax.rem(x + 4 - o, 4) * 32, 32)

    ring_slots = slots[0]
    slots[0] += 7

    def ring_copy(o, dst):
        at = ring_slots + o - 1
        return pltpu.make_async_remote_copy(
            src_ref=g_all.at[:, far, core, x, own8, :], dst_ref=dst, send_sem=send.at[at],
            recv_sem=recv.at[at], device_id=peer("ring", o), device_id_type=MESH,
        )

    def ring_start():
        @pl.when(slot < 3)
        def _():
            for o in range(1, 8):
                ring_copy(o, g_all.at[:, far, core, x, own8, :]).start()

    def ring_sent():
        @pl.when(slot < 3)
        def _():
            for o in range(1, 8):
                ring_copy(o, g_all.at[:, far, core, x, own8, :]).wait_send()

    def ring_wait(first):
        for o in range(1, 8):
            source_far, source = ring_source(o)

            @pl.when((source == 0) if first else ((source == 1) | (source == 2)))
            def _():
                rows = pl.ds(at8(source * 8), 8)
                ring_copy(o, g_all.at[:, source_far, core, x, rows, :]).wait_recv()

    def gather_rest(rows):
        along_x = exchange(
            "x",
            lambda o: g_all.at[:, :, core, x, rows, :],
            lambda o: g_all.at[:, :, core, x, rows, :],
            lambda o: g_all.at[:, :, core, lax.rem(x + 4 - o, 4), rows, :],
        )
        along_core = exchange(
            "core",
            lambda o: g_all.at[:, :, core, :, rows, :],
            lambda o: g_all.at[:, :, core, :, rows, :],
            lambda o: g_all.at[:, :, 1 - core, :, rows, :],
        )
        return along_x, along_core

    first_x, first_core = gather_rest(slice(0, 8))
    later_x, later_core = gather_rest(slice(8, 24))
    c_ring, cx, ccore, rz = {}, {}, {}, {}
    for h in halves:
        half = lanes[h]

        def c_landed(o, half=half):
            source_far, source = ring_source(o)
            rows = pl.ds(at8(core * 128 + x * 32 + source * 8), 8)
            return c_all.at[source_far, rows, half]

        c_ring[h] = exchange(
            "ring",
            lambda o, half=half: c_all.at[far, pl.ds(base, 8), half],
            lambda o, half=half: c_all.at[far, pl.ds(base, 8), half],
            c_landed,
        )
        cx[h] = exchange(
            "x",
            lambda o, half=half: c_all.at[:, pl.ds(row32(0), 32), half],
            lambda o, half=half: c_all.at[:, pl.ds(row32(0), 32), half],
            lambda o, half=half: c_all.at[:, pl.ds(row32(o), 32), half],
        )
        ccore[h] = exchange(
            "core",
            lambda o, half=half: c_all.at[:, pl.ds(at8(core * 128, 128), 128), half],
            lambda o, half=half: c_all.at[:, pl.ds(at8(core * 128, 128), 128), half],
            lambda o, half=half: c_all.at[:, pl.ds(at8((1 - core) * 128, 128), 128), half],
        )
        rz[h] = exchange(
            "z",
            lambda o, half=half: right.at[pl.ds(at8(lax.rem(z + o, 8) * 32, 32), 32), half],
            lambda o, half=half: from_z.at[o - 1, :, half],
            lambda o, half=half: from_z.at[o - 1, :, half],
        )

    def c_to_ring(h):
        stage[h, "y"][1]()
        c_all[far, pl.ds(base, 8), lanes[h]] = add_y(lanes[h])
        c_ring[h][0]()

    def c_gather_x(h):
        c_ring[h][1]()
        cx[h][0]()

    def c_gather_core(h):
        cx[h][1]()
        ccore[h][0]()

    gz[0]()
    c_to_y(0)
    c_to_y(1)
    gz[1]()
    ring_start()
    c_to_ring(0)
    c_to_ring(1)
    ring_wait(True)
    first_x[0]()
    ring_wait(False)
    later_x[0]()
    c_gather_x(0)
    first_x[1]()
    first_core[0]()
    c_gather_x(1)
    w_all[pl.ds(at8(z * 32, 32), 32), :] = weight[:, pl.ds(at8(z * 512, 512), 512)]
    ring_sent()
    first_core[1]()

    total = jnp.zeros((8, TILE), F32)
    for s in range(16):
        total = total + g_all[s // 2, s % 2, FIRST // 4, FIRST % 4, 0:8, :]
    total = jnp.sum(jnp.sum(total, axis=0, keepdims=True), axis=1, keepdims=True)
    damping = 0.01 * total / 4096.0

    def place(i, j, unit_at):
        rows, cols = slice(i * TILE, (i + 1) * TILE), slice(j * TILE, (j + 1) * TILE)
        for e in range(16):
            m[i * TILE + 8 * e : i * TILE + 8 * e + 8, cols] = unit_at(e)
        block = m[rows, cols]
        if i == j:
            eye = lax.broadcasted_iota(jnp.int32, (TILE, TILE), 0) == lax.broadcasted_iota(
                jnp.int32, (TILE, TILE), 1
            )
            m[rows, cols] = block + jnp.where(eye, damping, 0.0)
        else:
            m[cols, rows] = block.T

    for i in range(NBLOCK):

        def first_unit(e, i=i):
            s, u = divmod(i * 16 + e, FIRST)
            return g_all[s // 2, s % 2, u // 4, u % 4, 0:8, :]

        place(i, 0, first_unit)

    def later_blocks():
        later_x[1]()
        later_core[0]()
        later_core[1]()
        block = 0
        for i in range(1, NBLOCK):
            for j in range(1, i + 1):

                def later_unit(e, block=block):
                    s, u = divmod(block * 16 + e, LATER)
                    q = u % 8
                    at = 8 * (1 + u // 8)
                    return g_all[s // 2, s % 2, q // 4, q % 4, at : at + 8, :]

                place(i, j, later_unit)
                block += 1

    def right_side(h):
        ccore[h][1]()
        for b in range(2):
            high, middle, low = pieces(c_all[b, :, lanes[h]])
            w = w_all[:, b * 256 : (b + 1) * 256]
            term = jnp.dot(w, high, preferred_element_type=F32)
            term += jnp.dot(w, middle, preferred_element_type=F32)
            term += jnp.dot(w, low, preferred_element_type=F32)
            if b == 0:
                right[:, lanes[h]] = term
            else:
                right[:, lanes[h]] += term
        rz[h][0]()

    @pl.loop(0, NBLOCK)
    def _(k):
        @pl.when(k == 1)
        def _():
            c_gather_core(1)

        @pl.when(k == 2)
        def _():
            right_side(1)

        def arrive():
            @pl.when(k == 0)
            def _():
                later_blocks()
                c_gather_core(0)

            @pl.when(k == 1)
            def _():
                w_wait()
                right_side(0)

        eliminate(k, m, lower, n_tile, t_tile, scratch, left_pieces, right_pieces, arrive)

    rz[0][1]()
    rz[1][1]()
    own = right[pl.ds(at8(z * 32, 32), 32), :]
    for o in range(7):
        own = own + from_z[o]
    own = lax.dot_general(
        own, lower[...], (((1,), (1,)), ((), ())), precision=HIGHEST, preferred_element_type=F32
    )
    out[...] = jnp.dot(own, m[...], precision=HIGHEST, preferred_element_type=F32)


def spread_kernel(flags, solved, out):
    low = lax.broadcasted_iota(jnp.int32, (32, TILE), 1) < 64
    rank = jnp.int32(0)
    for g in range(32):
        sides = []
        for side in range(2):
            flag = flags[2 * g + side]
            at = jnp.minimum(rank, KEEP_BLK - 1)
            v = solved[:, pl.ds(pl.multiple_of((at // 2) * TILE, TILE), TILE)]
            v = jnp.where(at % 2 == side, v, _half_swap(v))
            sides.append(jnp.where(flag == 1, v, 0.0))
            rank = rank + flag
        out[:, g * TILE : (g + 1) * TILE] = jnp.where(low, sides[0], sides[1]).astype(BF16)


def on_device(tokens, orig_weight, keep_flags):
    vmem = pl.BlockSpec(memory_space=pltpu.VMEM)
    smem = pl.BlockSpec(memory_space=pltpu.SMEM)
    part = pl.pallas_call(
        prepare_kernel,
        out_shape=jax.ShapeDtypeStruct((256, WIDE), F32),
        in_specs=[smem, vmem],
        out_specs=vmem,
        scratch_shapes=[
            pltpu.SMEM((16,), jnp.int32),
            pltpu.VMEM((256, KEEP), BF16),
            pltpu.VMEM((KEEP, KEEP), F32),
        ],
        name="prepare",
    )(keep_flags, tokens)
    solved = pl.pallas_call(
        solve_kernel,
        out_shape=jax.ShapeDtypeStruct((32, KEEP), F32),
        in_specs=[vmem, vmem],
        out_specs=vmem,
        scratch_shapes=[
            pltpu.VMEM((128, WIDE), F32),
            pltpu.VMEM((3, 32, WIDE), F32),
            pltpu.VMEM((3, 8, WIDE), F32),
            pltpu.VMEM((128, WIDE), F32),
            pltpu.VMEM((32, WIDE), F32),
            pltpu.VMEM((8, 2, 2, 4, 32, TILE), F32),
            pltpu.VMEM((2, 256, KEEP), F32),
            pltpu.VMEM((256, 512), BF16),
            pltpu.VMEM((256, KEEP), F32),
            pltpu.VMEM((7, 32, KEEP), F32),
            pltpu.VMEM((KEEP, KEEP), F32),
            pltpu.VMEM((KEEP, KEEP), F32),
            pltpu.VMEM((TILE, TILE), F32),
            pltpu.VMEM((TILE, TILE), F32),
            pltpu.VMEM((8 * PANEL, TILE), F32),
            pltpu.VMEM((KEEP, KEEP), BF16),
            pltpu.VMEM((KEEP, KEEP), BF16),
            pltpu.SemaphoreType.DMA((96,)),
            pltpu.SemaphoreType.DMA((96,)),
        ],
        compiler_params=pltpu.CompilerParams(collective_id=0, has_side_effects=True),
        name="solve",
    )(part, orig_weight)
    return pl.pallas_call(
        spread_kernel,
        out_shape=jax.ShapeDtypeStruct((32, orig_weight.shape[1]), BF16),
        in_specs=[smem, vmem],
        out_specs=vmem,
        name="spread",
    )(keep_flags, solved)


def solution(mesh):
    in_specs = (P("dp", None), P(("section", "dp"), None), P())
    out_specs = P(("section", "dp"), None)
    return jax.shard_map(
        on_device, mesh=mesh, in_specs=in_specs, out_specs=out_specs, check_vma=False
    )
```

```python
import functools

import jax
import jax.numpy as jnp
from jax import lax
from jax.experimental import pallas as pl
from jax.experimental.pallas import tpu as pltpu
from jax.sharding import PartitionSpec as P

HIGHEST = lax.Precision.HIGHEST
F32 = jnp.float32
BF16 = jnp.bfloat16
MESH = pl.DeviceIdType.MESH

KEEP_BLK = 12
KEEP = 768
TILE = 128
PANEL = 8
NBLOCK = KEEP // TILE
FIRST = NBLOCK
LATER = NBLOCK * (NBLOCK - 1) // 2
WIDE = KEEP + TILE
CHUNK = 256


def _lower_block(t):
    row = jnp.int32(0)
    for i in range(1, NBLOCK - 1):
        row = row + (t >= i * (i + 1) // 2).astype(jnp.int32)
    return row, t - row * (row + 1) // 2


def _half_swap(v):
    return pltpu.roll(v, 64, 1)


def prepare_kernel(flags, tokens, part, kept, kept_tokens, gram):
    section = lax.axis_index("section")

    def note(b, count):
        kept[count] = b
        return count + flags[b]

    lax.fori_loop(0, 64, note, jnp.int32(0))
    low = lax.broadcasted_iota(jnp.int32, (256, TILE), 1) < 64
    for i in range(NBLOCK):
        first, second = kept[2 * i], kept[2 * i + 1]
        a = tokens[:, pl.ds(pl.multiple_of((first // 2) * TILE, TILE), TILE)].astype(F32)
        b = tokens[:, pl.ds(pl.multiple_of((second // 2) * TILE, TILE), TILE)].astype(F32)
        a = jnp.where(first % 2 == 1, _half_swap(a), a)
        b = jnp.where(second % 2 == 0, _half_swap(b), b)
        kept_tokens[:, i * TILE : (i + 1) * TILE] = jnp.where(low, a, b).astype(BF16)
    chunk = tokens[:, pl.ds(pl.multiple_of(section * CHUNK, CHUNK), CHUNK)]
    over_tokens = (((0,), (0,)), ((), ()))
    part[:, 0:KEEP] = lax.dot_general(
        chunk, kept_tokens[...], over_tokens, preferred_element_type=F32
    )
    gram[...] = lax.dot_general(
        kept_tokens[...], kept_tokens[...], over_tokens, preferred_element_type=F32
    )
    part[:, KEEP:WIDE] = jnp.zeros((256, TILE), F32)

    def put(at, unit, row, col):
        start = row * TILE + (unit % 16) * 8
        part[at : at + 8, KEEP:WIDE] = gram[
            pl.ds(pl.multiple_of(start, 8), 8), pl.ds(pl.multiple_of(col * TILE, TILE), TILE)
        ]

    for u in range(FIRST):
        unit = section * FIRST + u
        put(32 * u, unit, unit // 16, 0)
    for u in range(LATER):
        unit = section * LATER + u
        row, col = _lower_block(unit // 16)
        put(32 * (u % 8) + 8 * (1 + u // 8), unit, row + 1, col + 1)
    wide = chunk.astype(F32)
    squares = wide * wide
    squares = squares[:, :TILE] + squares[:, TILE:]
    total = squares[0:8]
    for g in range(1, 32):
        total = total + squares[8 * g : 8 * g + 8]
    part[32 * FIRST : 32 * FIRST + 8, KEEP:WIDE] = total


def tile_factors(rows, n, t, scratch):
    lane = lax.broadcasted_iota(jnp.int32, (8, TILE), 1)
    sub = lax.broadcasted_iota(jnp.int32, (8, TILE), 0)
    panels = TILE // PANEL
    rows = list(rows)

    def over_lanes(v, c):
        column = jnp.sum(jnp.where(lane == c, v, 0.0), axis=1, keepdims=True)
        return jnp.broadcast_to(column, (8, TILE))

    def over_rows(v, q):
        return jnp.broadcast_to(v[q : q + 1, :], (8, TILE))

    for c in range(PANEL):
        scratch[8 * c : 8 * c + 8, :] = over_lanes(rows[0], c)
    columns = [scratch[8 * c : 8 * c + 8, :] for c in range(PANEL)]
    for j in range(panels):
        base = j * PANEL
        more = j + 1 < panels
        if more:
            ahead = [over_lanes(rows[j], base + PANEL + c) for c in range(PANEL)]
            below = [over_lanes(rows[j + 1], base + c) for c in range(PANEL)]
            coming = [over_lanes(rows[j + 1], base + PANEL + c) for c in range(PANEL)]
        inside = (lane >= base) & (lane < base + PANEL)
        r = jnp.where(inside, (lane - base == sub).astype(F32), rows[j])
        n[base : base + 8, :] = jnp.where(lane < base + PANEL, r, 0.0)
        for q in range(PANEL):
            inv = 1.0 / over_rows(columns[q], q)
            pivot = sub == q
            m = jnp.where(pivot, 0.0, columns[q] * inv)
            scale = jnp.where(pivot, inv, 1.0)
            r = r * scale - m * over_rows(r, q)
            for c in range(q + 1, PANEL):
                columns[c] = columns[c] * scale - m * over_rows(columns[c], q)
            if more:
                for c in range(PANEL):
                    ahead[c] = ahead[c] * scale - m * over_rows(ahead[c], q)
        t[base : base + 8, :] = jnp.where(lane < base + PANEL, r, 0.0)
        if more:
            columns = []
            for c in range(PANEL):
                terms = [below[q] * over_rows(ahead[c], q) for q in range(PANEL)]
                while len(terms) > 1:
                    terms = [a + b for a, b in zip(terms[::2], terms[1::2])]
                columns.append(coming[c] - terms[0])
        spread = [over_rows(r, c) for c in range(PANEL)]
        for g in range(j + 1, panels):
            acc = jnp.where(inside, 0.0, rows[g])
            for c in range(PANEL):
                factor = below[c] if g == j + 1 else over_lanes(rows[g], base + c)
                acc = acc - factor * spread[c]
            rows[g] = acc


def pieces(v):
    high = v.astype(BF16)
    v = v - high.astype(F32)
    middle = v.astype(BF16)
    return high, middle, (v - middle.astype(F32)).astype(BF16)


def put_left(ref, rows, v):
    high, middle, low = pieces(v)
    for i, p in enumerate((high, high, middle, middle, high, low)):
        ref[rows, i * TILE : (i + 1) * TILE] = p


def put_right(ref, v):
    high, middle, low = pieces(v)
    for i, p in enumerate((high, middle, high, middle, low, high)):
        ref[i * TILE : (i + 1) * TILE, :] = p


def eliminate(k, m, lower, n, t, scratch, left, right, arrive):
    off = pl.multiple_of(k * TILE, TILE)
    rows = [m[pl.ds(pl.multiple_of(off + 8 * g, 8), 8), pl.ds(off, TILE)] for g in range(TILE // 8)]
    tile_factors(rows, n, t, scratch)
    arrive()
    d = lax.dot_general(
        n[...], t[...], (((0,), (0,)), ((), ())), precision=HIGHEST, preferred_element_type=F32
    )
    col = lax.broadcasted_iota(jnp.int32, (TILE, KEEP), 1) - off
    row = lax.broadcasted_iota(jnp.int32, (TILE, KEEP), 0)
    inside = (col >= 0) & (col < TILE)
    r = jnp.where(inside, (col == row).astype(F32), m[pl.ds(off, TILE), :])
    lower[pl.ds(off, TILE), :] = jnp.where(col < TILE, r, 0.0)
    put_left(left, slice(0, TILE), d)
    put_right(right, r)
    r = jnp.dot(left[0:TILE, :], right[...], preferred_element_type=F32)
    m[pl.ds(off, TILE), :] = jnp.where(col < TILE, r, 0.0)
    put_right(right, r)
    for kk in range(NBLOCK - 1):

        @pl.when(k == kk)
        def _():
            start = kk * TILE
            stop = start + TILE
            put_left(left, slice(stop, KEEP), m[stop:KEEP, start:stop])
            p = jnp.dot(left[stop:KEEP, :], right[...], preferred_element_type=F32)
            if kk:
                m[stop:KEEP, 0:start] = m[stop:KEEP, 0:start] - p[:, 0:start]
            m[stop:KEEP, start:stop] = -p[:, start:stop]
            m[stop:KEEP, stop:KEEP] = m[stop:KEEP, stop:KEEP] - p[:, stop:KEEP]


def solve_kernel(
    part, weight, out,
    from_core, from_x, from_y, sums, shares, g_all, c_all, w_all, right, from_z,
    m, lower, n_tile, t_tile, scratch, left_pieces, right_pieces, send, recv,
):
    section, dp = lax.axis_index("section"), lax.axis_index("dp")
    z, far = section // 2, section % 2
    x, y, core = dp // 8, (dp // 2) % 4, dp % 2
    slot = lax.rem(y + 3, 4)

    def peer(axis, o):
        if axis == "z":
            return (lax.rem(z + o, 8) * 2 + far, dp)
        if axis == "ring":
            at = lax.rem(far * 4 + y + o, 8)
            return (z * 2 + at // 4, x * 8 + lax.rem(at, 4) * 2 + core)
        if axis == "x":
            return (section, lax.rem(x + o, 4) * 8 + y * 2 + core)
        if axis == "y":
            return (section, x * 8 + lax.rem(y + o, 4) * 2 + core)
        return (section, x * 8 + y * 2 + 1 - core)

    sizes = {"z": 8, "ring": 8, "x": 4, "y": 4, "core": 2}
    barrier = pltpu.get_barrier_semaphore()
    greeted = 0
    for axis in ("z", "ring", "x", "core"):
        for o in range(1, sizes[axis]):
            pl.semaphore_signal(barrier, inc=1, device_id=peer(axis, o), device_id_type=MESH)
            greeted += 1
    pl.semaphore_wait(barrier, greeted)

    slots = [0]

    def exchange(axis, source, target, landed):
        first = slots[0]
        n = sizes[axis]
        slots[0] += n - 1

        def copy(o, dst):
            at = first + o - 1
            return pltpu.make_async_remote_copy(
                src_ref=source(o), dst_ref=dst, send_sem=send.at[at], recv_sem=recv.at[at],
                device_id=peer(axis, o), device_id_type=MESH,
            )

        def start():
            for o in range(1, n):
                copy(o, target(o)).start()

        def wait():
            for o in range(1, n):
                copy(o, landed(o)).wait_send()
            for o in range(1, n):
                copy(o, landed(o)).wait_recv()

        return start, wait

    def at8(v, n=8):
        return pl.multiple_of(v, n)

    w_start, w_wait = exchange(
        "z",
        lambda o: weight.at[:, pl.ds(at8(lax.rem(z + o, 8) * 512, 512), 512)],
        lambda o: w_all.at[pl.ds(at8(z * 32, 32), 32), :],
        lambda o: w_all.at[pl.ds(at8(lax.rem(z + 8 - o, 8) * 32, 32), 32), :],
    )
    w_start()

    thirds = (0, 1, 2)
    lanes = {"g": slice(KEEP, WIDE)}
    for h in thirds:
        lanes[h] = slice(h * KEEP // 3, (h + 1) * KEEP // 3)
    stage = {}
    for name in ("g", *thirds):
        cut = lanes[name]
        stage[name, "core"] = exchange(
            "core",
            lambda o, cut=cut: part.at[pl.ds(at8((1 - core) * 128, 128), 128), cut],
            lambda o, cut=cut: from_core.at[:, cut],
            lambda o, cut=cut: from_core.at[:, cut],
        )
        stage[name, "x"] = exchange(
            "x",
            lambda o, cut=cut: sums.at[pl.ds(at8(lax.rem(x + o, 4) * 32, 32), 32), cut],
            lambda o, cut=cut: from_x.at[o - 1, :, cut],
            lambda o, cut=cut: from_x.at[o - 1, :, cut],
        )
        stage[name, "y"] = exchange(
            "y",
            lambda o, cut=cut: shares.at[pl.ds(at8(lax.rem(slot + o, 4) * 8), 8), cut],
            lambda o, cut=cut: from_y.at[o - 1, :, cut],
            lambda o, cut=cut: from_y.at[o - 1, :, cut],
        )

    def add_core(cut):
        sums[:, cut] = part[pl.ds(at8(core * 128, 128), 128), cut] + from_core[:, cut]

    def add_x(cut):
        own = sums[pl.ds(at8(x * 32, 32), 32), cut]
        shares[:, cut] = own + from_x[0, :, cut] + from_x[1, :, cut] + from_x[2, :, cut]

    def add_y(cut):
        own = shares[pl.ds(at8(slot * 8), 8), cut]
        return own + from_y[0, :, cut] + from_y[1, :, cut] + from_y[2, :, cut]

    base = at8(core * 128 + x * 32 + slot * 8)
    g_cut = lanes["g"]
    stage["g", "core"][0]()
    for h in thirds:
        stage[h, "core"][0]()

    def c_to_x(h):
        stage[h, "core"][1]()
        add_core(lanes[h])
        stage[h, "x"][0]()

    def c_to_y(h):
        stage[h, "x"][1]()
        add_x(lanes[h])
        stage[h, "y"][0]()

    stage["g", "core"][1]()
    add_core(g_cut)
    stage["g", "x"][0]()
    c_to_x(0)
    stage["g", "x"][1]()
    add_x(g_cut)
    stage["g", "y"][0]()
    c_to_x(1)
    c_to_x(2)
    stage["g", "y"][1]()
    own8 = pl.ds(at8(slot * 8), 8)
    g_all[z, far, core, x, own8, :] = add_y(g_cut)

    gz = exchange(
        "z",
        lambda o: g_all.at[z, far, core, x, own8, :],
        lambda o: g_all.at[z, far, core, x, own8, :],
        lambda o: g_all.at[lax.rem(z + 8 - o, 8), far, core, x, own8, :],
    )
    def ring_source(o):
        at = lax.rem(far * 4 + y + 8 - o, 8)
        return at // 4, lax.rem(at + 3, 4)

    def row32(o):
        return at8(core * 128 + lax.rem(x + 4 - o, 4) * 32, 32)

    ring_slots = slots[0]
    slots[0] += 7

    def ring_copy(o, dst):
        at = ring_slots + o - 1
        return pltpu.make_async_remote_copy(
            src_ref=g_all.at[:, far, core, x, own8, :], dst_ref=dst, send_sem=send.at[at],
            recv_sem=recv.at[at], device_id=peer("ring", o), device_id_type=MESH,
        )

    def ring_start():
        @pl.when(slot < 3)
        def _():
            for o in range(1, 8):
                ring_copy(o, g_all.at[:, far, core, x, own8, :]).start()

    def ring_sent():
        @pl.when(slot < 3)
        def _():
            for o in range(1, 8):
                ring_copy(o, g_all.at[:, far, core, x, own8, :]).wait_send()

    def ring_wait(first):
        for o in range(1, 8):
            source_far, source = ring_source(o)

            @pl.when((source == 0) if first else ((source == 1) | (source == 2)))
            def _():
                rows = pl.ds(at8(source * 8), 8)
                ring_copy(o, g_all.at[:, source_far, core, x, rows, :]).wait_recv()

    def gather_rest(rows):
        along_x = exchange(
            "x",
            lambda o: g_all.at[:, :, core, x, rows, :],
            lambda o: g_all.at[:, :, core, x, rows, :],
            lambda o: g_all.at[:, :, core, lax.rem(x + 4 - o, 4), rows, :],
        )
        along_core = exchange(
            "core",
            lambda o: g_all.at[:, :, core, :, rows, :],
            lambda o: g_all.at[:, :, core, :, rows, :],
            lambda o: g_all.at[:, :, 1 - core, :, rows, :],
        )
        return along_x, along_core

    first_x, first_core = gather_rest(slice(0, 8))
    later_x, later_core = gather_rest(slice(8, 24))
    c_ring, cx, ccore, rz = {}, {}, {}, {}
    for h in thirds:
        third = lanes[h]

        def c_landed(o, third=third):
            source_far, source = ring_source(o)
            rows = pl.ds(at8(core * 128 + x * 32 + source * 8), 8)
            return c_all.at[source_far, rows, third]

        c_ring[h] = exchange(
            "ring",
            lambda o, third=third: c_all.at[far, pl.ds(base, 8), third],
            lambda o, third=third: c_all.at[far, pl.ds(base, 8), third],
            c_landed,
        )
        cx[h] = exchange(
            "x",
            lambda o, third=third: c_all.at[:, pl.ds(row32(0), 32), third],
            lambda o, third=third: c_all.at[:, pl.ds(row32(0), 32), third],
            lambda o, third=third: c_all.at[:, pl.ds(row32(o), 32), third],
        )
        ccore[h] = exchange(
            "core",
            lambda o, third=third: c_all.at[:, pl.ds(at8(core * 128, 128), 128), third],
            lambda o, third=third: c_all.at[:, pl.ds(at8(core * 128, 128), 128), third],
            lambda o, third=third: c_all.at[:, pl.ds(at8((1 - core) * 128, 128), 128), third],
        )
        rz[h] = exchange(
            "z",
            lambda o, third=third: right.at[pl.ds(at8(lax.rem(z + o, 8) * 32, 32), 32), third],
            lambda o, third=third: from_z.at[o - 1, :, third],
            lambda o, third=third: from_z.at[o - 1, :, third],
        )

    def c_to_ring(h):
        stage[h, "y"][1]()
        c_all[far, pl.ds(base, 8), lanes[h]] = add_y(lanes[h])
        c_ring[h][0]()

    def c_gather_x(h):
        c_ring[h][1]()
        cx[h][0]()

    def c_gather_core(h):
        cx[h][1]()
        ccore[h][0]()

    gz[0]()
    for h in thirds:
        c_to_y(h)
    gz[1]()
    ring_start()
    for h in thirds:
        c_to_ring(h)
    ring_wait(True)
    first_x[0]()
    c_gather_x(0)
    ring_wait(False)
    later_x[0]()
    first_x[1]()
    first_core[0]()
    c_gather_x(1)
    c_gather_x(2)
    w_all[pl.ds(at8(z * 32, 32), 32), :] = weight[:, pl.ds(at8(z * 512, 512), 512)]
    ring_sent()
    first_core[1]()

    total = jnp.zeros((8, TILE), F32)
    for s in range(16):
        total = total + g_all[s // 2, s % 2, FIRST // 4, FIRST % 4, 0:8, :]
    total = jnp.sum(jnp.sum(total, axis=0, keepdims=True), axis=1, keepdims=True)
    damping = 0.01 * total / 4096.0

    def place(i, j, unit_at):
        rows, cols = slice(i * TILE, (i + 1) * TILE), slice(j * TILE, (j + 1) * TILE)
        for e in range(16):
            m[i * TILE + 8 * e : i * TILE + 8 * e + 8, cols] = unit_at(e)
        block = m[rows, cols]
        if i == j:
            eye = lax.broadcasted_iota(jnp.int32, (TILE, TILE), 0) == lax.broadcasted_iota(
                jnp.int32, (TILE, TILE), 1
            )
            m[rows, cols] = block + jnp.where(eye, damping, 0.0)
        else:
            m[cols, rows] = block.T

    for i in range(NBLOCK):

        def first_unit(e, i=i):
            s, u = divmod(i * 16 + e, FIRST)
            return g_all[s // 2, s % 2, u // 4, u % 4, 0:8, :]

        place(i, 0, first_unit)

    def later_blocks():
        c_gather_core(0)
        later_x[1]()
        later_core[0]()
        c_gather_core(1)
        later_core[1]()
        block = 0
        for i in range(1, NBLOCK):
            for j in range(1, i + 1):

                def later_unit(e, block=block):
                    s, u = divmod(block * 16 + e, LATER)
                    q = u % 8
                    at = 8 * (1 + u // 8)
                    return g_all[s // 2, s % 2, q // 4, q % 4, at : at + 8, :]

                place(i, j, later_unit)
                block += 1

    def right_side(h):
        ccore[h][1]()
        for b in range(2):
            high, middle, low = pieces(c_all[b, :, lanes[h]])
            w = w_all[:, b * 256 : (b + 1) * 256]
            term = jnp.dot(w, high, preferred_element_type=F32)
            term += jnp.dot(w, middle, preferred_element_type=F32)
            term += jnp.dot(w, low, preferred_element_type=F32)
            if b == 0:
                right[:, lanes[h]] = term
            else:
                right[:, lanes[h]] += term
        rz[h][0]()

    @pl.loop(0, NBLOCK)
    def _(k):
        @pl.when(k == 1)
        def _():
            w_wait()
            right_side(0)
            c_gather_core(2)

        @pl.when(k == 2)
        def _():
            right_side(2)

        def arrive():
            @pl.when(k == 0)
            def _():
                later_blocks()

            @pl.when(k == 1)
            def _():
                right_side(1)

        eliminate(k, m, lower, n_tile, t_tile, scratch, left_pieces, right_pieces, arrive)

    for h in thirds:
        rz[h][1]()
    own = right[pl.ds(at8(z * 32, 32), 32), :]
    for o in range(7):
        own = own + from_z[o]
    own = lax.dot_general(
        own, lower[...], (((1,), (1,)), ((), ())), precision=HIGHEST, preferred_element_type=F32
    )
    out[...] = jnp.dot(own, m[...], precision=HIGHEST, preferred_element_type=F32)


def spread_kernel(flags, solved, out):
    low = lax.broadcasted_iota(jnp.int32, (32, TILE), 1) < 64
    rank = jnp.int32(0)
    for g in range(32):
        sides = []
        for side in range(2):
            flag = flags[2 * g + side]
            at = jnp.minimum(rank, KEEP_BLK - 1)
            v = solved[:, pl.ds(pl.multiple_of((at // 2) * TILE, TILE), TILE)]
            v = jnp.where(at % 2 == side, v, _half_swap(v))
            sides.append(jnp.where(flag == 1, v, 0.0))
            rank = rank + flag
        out[:, g * TILE : (g + 1) * TILE] = jnp.where(low, sides[0], sides[1]).astype(BF16)


def on_device(tokens, orig_weight, keep_flags):
    vmem = pl.BlockSpec(memory_space=pltpu.VMEM)
    smem = pl.BlockSpec(memory_space=pltpu.SMEM)
    part = pl.pallas_call(
        prepare_kernel,
        out_shape=jax.ShapeDtypeStruct((256, WIDE), F32),
        in_specs=[smem, vmem],
        out_specs=vmem,
        scratch_shapes=[
            pltpu.SMEM((16,), jnp.int32),
            pltpu.VMEM((256, KEEP), BF16),
            pltpu.VMEM((KEEP, KEEP), F32),
        ],
        name="prepare",
    )(keep_flags, tokens)
    solved = pl.pallas_call(
        solve_kernel,
        out_shape=jax.ShapeDtypeStruct((32, KEEP), F32),
        in_specs=[vmem, vmem],
        out_specs=vmem,
        scratch_shapes=[
            pltpu.VMEM((128, WIDE), F32),
            pltpu.VMEM((3, 32, WIDE), F32),
            pltpu.VMEM((3, 8, WIDE), F32),
            pltpu.VMEM((128, WIDE), F32),
            pltpu.VMEM((32, WIDE), F32),
            pltpu.VMEM((8, 2, 2, 4, 32, TILE), F32),
            pltpu.VMEM((2, 256, KEEP), F32),
            pltpu.VMEM((256, 512), BF16),
            pltpu.VMEM((256, KEEP), F32),
            pltpu.VMEM((7, 32, KEEP), F32),
            pltpu.VMEM((KEEP, KEEP), F32),
            pltpu.VMEM((KEEP, KEEP), F32),
            pltpu.VMEM((TILE, TILE), F32),
            pltpu.VMEM((TILE, TILE), F32),
            pltpu.VMEM((8 * PANEL, TILE), F32),
            pltpu.VMEM((KEEP, KEEP), BF16),
            pltpu.VMEM((KEEP, KEEP), BF16),
            pltpu.SemaphoreType.DMA((128,)),
            pltpu.SemaphoreType.DMA((128,)),
        ],
        compiler_params=pltpu.CompilerParams(collective_id=0, has_side_effects=True),
        name="solve",
    )(part, orig_weight)
    return pl.pallas_call(
        spread_kernel,
        out_shape=jax.ShapeDtypeStruct((32, orig_weight.shape[1]), BF16),
        in_specs=[smem, vmem],
        out_specs=vmem,
        name="spread",
    )(keep_flags, solved)


def solution(mesh):
    in_specs = (P("dp", None), P(("section", "dp"), None), P())
    out_specs = P(("section", "dp"), None)
    return jax.shard_map(
        on_device, mesh=mesh, in_specs=in_specs, out_specs=out_specs, check_vma=False
    )
```

```python
import functools

import jax
import jax.numpy as jnp
from jax import lax
from jax.experimental import pallas as pl
from jax.experimental.pallas import tpu as pltpu
from jax.sharding import PartitionSpec as P

HIGHEST = lax.Precision.HIGHEST
F32 = jnp.float32
BF16 = jnp.bfloat16
MESH = pl.DeviceIdType.MESH

KEEP_BLK = 12
KEEP = 768
TILE = 128
PANEL = 8
NBLOCK = KEEP // TILE
FIRST = NBLOCK
LATER = NBLOCK * (NBLOCK - 1) // 2
WIDE = KEEP + TILE
CHUNK = 256


def _lower_block(t):
    row = jnp.int32(0)
    for i in range(1, NBLOCK - 1):
        row = row + (t >= i * (i + 1) // 2).astype(jnp.int32)
    return row, t - row * (row + 1) // 2


def _half_swap(v):
    return pltpu.roll(v, 64, 1)


def prepare_kernel(flags, tokens, part, kept, kept_tokens, gram):
    section = lax.axis_index("section")

    count = jnp.int32(0)
    for b in range(64):
        kept[count] = b
        count = count + flags[b]
    low = lax.broadcasted_iota(jnp.int32, (256, TILE), 1) < 64
    for i in range(NBLOCK):
        first, second = kept[2 * i], kept[2 * i + 1]
        a = tokens[:, pl.ds(pl.multiple_of((first // 2) * TILE, TILE), TILE)].astype(F32)
        b = tokens[:, pl.ds(pl.multiple_of((second // 2) * TILE, TILE), TILE)].astype(F32)
        a = jnp.where(first % 2 == 1, _half_swap(a), a)
        b = jnp.where(second % 2 == 0, _half_swap(b), b)
        kept_tokens[:, i * TILE : (i + 1) * TILE] = jnp.where(low, a, b).astype(BF16)
    chunk = tokens[:, pl.ds(pl.multiple_of(section * CHUNK, CHUNK), CHUNK)]
    over_tokens = (((0,), (0,)), ((), ()))
    part[:, 0:KEEP] = lax.dot_general(
        chunk, kept_tokens[...], over_tokens, preferred_element_type=F32
    )
    gram[...] = lax.dot_general(
        kept_tokens[...], kept_tokens[...], over_tokens, preferred_element_type=F32
    )
    part[:, KEEP:WIDE] = jnp.zeros((256, TILE), F32)

    def put(at, unit, row, col):
        start = row * TILE + (unit % 16) * 8
        part[at : at + 8, KEEP:WIDE] = gram[
            pl.ds(pl.multiple_of(start, 8), 8), pl.ds(pl.multiple_of(col * TILE, TILE), TILE)
        ]

    for u in range(FIRST):
        unit = section * FIRST + u
        put(32 * u, unit, unit // 16, 0)
    for u in range(LATER):
        unit = section * LATER + u
        row, col = _lower_block(unit // 16)
        put(32 * (u % 8) + 8 * (1 + u // 8), unit, row + 1, col + 1)
    wide = chunk.astype(F32)
    squares = wide * wide
    squares = squares[:, :TILE] + squares[:, TILE:]
    total = squares[0:8]
    for g in range(1, 32):
        total = total + squares[8 * g : 8 * g + 8]
    part[32 * FIRST : 32 * FIRST + 8, KEEP:WIDE] = total


def tile_factors(rows, n, t, scratch):
    lane = lax.broadcasted_iota(jnp.int32, (8, TILE), 1)
    sub = lax.broadcasted_iota(jnp.int32, (8, TILE), 0)
    panels = TILE // PANEL
    rows = list(rows)

    def over_lanes(v, c):
        column = jnp.sum(jnp.where(lane == c, v, 0.0), axis=1, keepdims=True)
        return jnp.broadcast_to(column, (8, TILE))

    def over_rows(v, q):
        return jnp.broadcast_to(v[q : q + 1, :], (8, TILE))

    for c in range(PANEL):
        scratch[8 * c : 8 * c + 8, :] = over_lanes(rows[0], c)
    columns = [scratch[8 * c : 8 * c + 8, :] for c in range(PANEL)]
    for j in range(panels):
        base = j * PANEL
        more = j + 1 < panels
        if more:
            ahead = [over_lanes(rows[j], base + PANEL + c) for c in range(PANEL)]
            below = [over_lanes(rows[j + 1], base + c) for c in range(PANEL)]
            coming = [over_lanes(rows[j + 1], base + PANEL + c) for c in range(PANEL)]
        inside = (lane >= base) & (lane < base + PANEL)
        r = jnp.where(inside, (lane - base == sub).astype(F32), rows[j])
        n[base : base + 8, :] = jnp.where(lane < base + PANEL, r, 0.0)
        for q in range(PANEL):
            inv = 1.0 / over_rows(columns[q], q)
            pivot = sub == q
            m = jnp.where(pivot, 0.0, columns[q] * inv)
            scale = jnp.where(pivot, inv, 1.0)
            r = r * scale - m * over_rows(r, q)
            for c in range(q + 1, PANEL):
                columns[c] = columns[c] * scale - m * over_rows(columns[c], q)
            if more:
                for c in range(PANEL):
                    ahead[c] = ahead[c] * scale - m * over_rows(ahead[c], q)
        t[base : base + 8, :] = jnp.where(lane < base + PANEL, r, 0.0)
        if more:
            columns = []
            for c in range(PANEL):
                terms = [below[q] * over_rows(ahead[c], q) for q in range(PANEL)]
                while len(terms) > 1:
                    terms = [a + b for a, b in zip(terms[::2], terms[1::2])]
                columns.append(coming[c] - terms[0])
        spread = [over_rows(r, c) for c in range(PANEL)]
        for g in range(j + 1, panels):
            acc = jnp.where(inside, 0.0, rows[g])
            for c in range(PANEL):
                factor = below[c] if g == j + 1 else over_lanes(rows[g], base + c)
                acc = acc - factor * spread[c]
            rows[g] = acc


def pieces(v):
    high = v.astype(BF16)
    v = v - high.astype(F32)
    middle = v.astype(BF16)
    return high, middle, (v - middle.astype(F32)).astype(BF16)


def put_left(ref, rows, v):
    high, middle, low = pieces(v)
    for i, p in enumerate((high, high, middle, middle, high, low)):
        ref[rows, i * TILE : (i + 1) * TILE] = p


def put_right(ref, v):
    high, middle, low = pieces(v)
    for i, p in enumerate((high, middle, high, middle, low, high)):
        ref[i * TILE : (i + 1) * TILE, :] = p


def eliminate(k, m, lower, n, t, scratch, left, right, arrive):
    off = pl.multiple_of(k * TILE, TILE)
    rows = [m[pl.ds(pl.multiple_of(off + 8 * g, 8), 8), pl.ds(off, TILE)] for g in range(TILE // 8)]
    tile_factors(rows, n, t, scratch)
    arrive()
    d = lax.dot_general(
        n[...], t[...], (((0,), (0,)), ((), ())), precision=HIGHEST, preferred_element_type=F32
    )
    col = lax.broadcasted_iota(jnp.int32, (TILE, KEEP), 1) - off
    row = lax.broadcasted_iota(jnp.int32, (TILE, KEEP), 0)
    inside = (col >= 0) & (col < TILE)
    r = jnp.where(inside, (col == row).astype(F32), m[pl.ds(off, TILE), :])
    lower[pl.ds(off, TILE), :] = jnp.where(col < TILE, r, 0.0)
    put_left(left, slice(0, TILE), d)
    put_right(right, r)
    r = jnp.dot(left[0:TILE, :], right[...], preferred_element_type=F32)
    m[pl.ds(off, TILE), :] = jnp.where(col < TILE, r, 0.0)
    put_right(right, r)
    for kk in range(NBLOCK - 1):

        @pl.when(k == kk)
        def _():
            start = kk * TILE
            stop = start + TILE
            put_left(left, slice(stop, KEEP), m[stop:KEEP, start:stop])
            p = jnp.dot(left[stop:KEEP, :], right[...], preferred_element_type=F32)
            if kk:
                m[stop:KEEP, 0:start] = m[stop:KEEP, 0:start] - p[:, 0:start]
            m[stop:KEEP, start:stop] = -p[:, start:stop]
            m[stop:KEEP, stop:KEEP] = m[stop:KEEP, stop:KEEP] - p[:, stop:KEEP]


def solve_kernel(
    part, weight, out,
    from_core, from_x, from_y, sums, shares, g_all, c_all, w_all, right, from_z,
    m, lower, n_tile, t_tile, scratch, left_pieces, right_pieces, lower_pieces, m_pieces, send, recv,
):
    section, dp = lax.axis_index("section"), lax.axis_index("dp")
    z, far = section // 2, section % 2
    x, y, core = dp // 8, (dp // 2) % 4, dp % 2
    slot = lax.rem(y + 3, 4)

    def peer(axis, o):
        if axis == "z":
            return (lax.rem(z + o, 8) * 2 + far, dp)
        if axis == "ring":
            at = lax.rem(far * 4 + y + o, 8)
            return (z * 2 + at // 4, x * 8 + lax.rem(at, 4) * 2 + core)
        if axis == "x":
            return (section, lax.rem(x + o, 4) * 8 + y * 2 + core)
        if axis == "y":
            return (section, x * 8 + lax.rem(y + o, 4) * 2 + core)
        return (section, x * 8 + y * 2 + 1 - core)

    sizes = {"z": 8, "ring": 8, "x": 4, "y": 4, "core": 2}
    barrier = pltpu.get_barrier_semaphore()
    greeted = 0
    for axis in ("z", "ring", "x", "core"):
        for o in range(1, sizes[axis]):
            pl.semaphore_signal(barrier, inc=1, device_id=peer(axis, o), device_id_type=MESH)
            greeted += 1
    pl.semaphore_wait(barrier, greeted)

    slots = [0]

    def exchange(axis, source, target, landed):
        first = slots[0]
        n = sizes[axis]
        slots[0] += n - 1

        def copy(o, dst):
            at = first + o - 1
            return pltpu.make_async_remote_copy(
                src_ref=source(o), dst_ref=dst, send_sem=send.at[at], recv_sem=recv.at[at],
                device_id=peer(axis, o), device_id_type=MESH,
            )

        def start():
            for o in range(1, n):
                copy(o, target(o)).start()

        def wait():
            for o in range(1, n):
                copy(o, landed(o)).wait_send()
            for o in range(1, n):
                copy(o, landed(o)).wait_recv()

        return start, wait

    def at8(v, n=8):
        return pl.multiple_of(v, n)

    w_start, w_wait = exchange(
        "z",
        lambda o: weight.at[:, pl.ds(at8(lax.rem(z + o, 8) * 512, 512), 512)],
        lambda o: w_all.at[pl.ds(at8(z * 32, 32), 32), :],
        lambda o: w_all.at[pl.ds(at8(lax.rem(z + 8 - o, 8) * 32, 32), 32), :],
    )
    w_start()

    thirds = (0, 1, 2)
    lanes = {"g": slice(KEEP, WIDE)}
    for h in thirds:
        lanes[h] = slice(h * KEEP // 3, (h + 1) * KEEP // 3)
    stage = {}
    for name in ("g", *thirds):
        cut = lanes[name]
        stage[name, "core"] = exchange(
            "core",
            lambda o, cut=cut: part.at[pl.ds(at8((1 - core) * 128, 128), 128), cut],
            lambda o, cut=cut: from_core.at[:, cut],
            lambda o, cut=cut: from_core.at[:, cut],
        )
        stage[name, "x"] = exchange(
            "x",
            lambda o, cut=cut: sums.at[pl.ds(at8(lax.rem(x + o, 4) * 32, 32), 32), cut],
            lambda o, cut=cut: from_x.at[o - 1, :, cut],
            lambda o, cut=cut: from_x.at[o - 1, :, cut],
        )
        stage[name, "y"] = exchange(
            "y",
            lambda o, cut=cut: shares.at[pl.ds(at8(lax.rem(slot + o, 4) * 8), 8), cut],
            lambda o, cut=cut: from_y.at[o - 1, :, cut],
            lambda o, cut=cut: from_y.at[o - 1, :, cut],
        )

    def add_core(cut):
        sums[:, cut] = part[pl.ds(at8(core * 128, 128), 128), cut] + from_core[:, cut]

    def add_x(cut):
        own = sums[pl.ds(at8(x * 32, 32), 32), cut]
        shares[:, cut] = own + from_x[0, :, cut] + from_x[1, :, cut] + from_x[2, :, cut]

    def add_y(cut):
        own = shares[pl.ds(at8(slot * 8), 8), cut]
        return own + from_y[0, :, cut] + from_y[1, :, cut] + from_y[2, :, cut]

    base = at8(core * 128 + x * 32 + slot * 8)
    g_cut = lanes["g"]
    stage["g", "core"][0]()
    for h in thirds:
        stage[h, "core"][0]()

    def c_to_x(h):
        stage[h, "core"][1]()
        add_core(lanes[h])
        stage[h, "x"][0]()

    def c_to_y(h):
        stage[h, "x"][1]()
        add_x(lanes[h])
        stage[h, "y"][0]()

    stage["g", "core"][1]()
    add_core(g_cut)
    stage["g", "x"][0]()
    c_to_x(0)
    stage["g", "x"][1]()
    add_x(g_cut)
    stage["g", "y"][0]()
    c_to_x(1)
    c_to_x(2)
    stage["g", "y"][1]()
    own8 = pl.ds(at8(slot * 8), 8)
    g_all[z, far, core, x, own8, :] = add_y(g_cut)

    gz = exchange(
        "z",
        lambda o: g_all.at[z, far, core, x, own8, :],
        lambda o: g_all.at[z, far, core, x, own8, :],
        lambda o: g_all.at[lax.rem(z + 8 - o, 8), far, core, x, own8, :],
    )
    def ring_source(o):
        at = lax.rem(far * 4 + y + 8 - o, 8)
        return at // 4, lax.rem(at + 3, 4)

    def row32(o):
        return at8(core * 128 + lax.rem(x + 4 - o, 4) * 32, 32)

    ring_slots = slots[0]
    slots[0] += 7

    def ring_copy(o, dst):
        at = ring_slots + o - 1
        return pltpu.make_async_remote_copy(
            src_ref=g_all.at[:, far, core, x, own8, :], dst_ref=dst, send_sem=send.at[at],
            recv_sem=recv.at[at], device_id=peer("ring", o), device_id_type=MESH,
        )

    def ring_start():
        @pl.when(slot < 3)
        def _():
            for o in range(1, 8):
                ring_copy(o, g_all.at[:, far, core, x, own8, :]).start()

    def ring_sent():
        @pl.when(slot < 3)
        def _():
            for o in range(1, 8):
                ring_copy(o, g_all.at[:, far, core, x, own8, :]).wait_send()

    def ring_wait(first):
        for o in range(1, 8):
            source_far, source = ring_source(o)

            @pl.when((source == 0) if first else ((source == 1) | (source == 2)))
            def _():
                rows = pl.ds(at8(source * 8), 8)
                ring_copy(o, g_all.at[:, source_far, core, x, rows, :]).wait_recv()

    def gather_rest(rows):
        along_x = exchange(
            "x",
            lambda o: g_all.at[:, :, core, x, rows, :],
            lambda o: g_all.at[:, :, core, x, rows, :],
            lambda o: g_all.at[:, :, core, lax.rem(x + 4 - o, 4), rows, :],
        )
        along_core = exchange(
            "core",
            lambda o: g_all.at[:, :, core, :, rows, :],
            lambda o: g_all.at[:, :, core, :, rows, :],
            lambda o: g_all.at[:, :, 1 - core, :, rows, :],
        )
        return along_x, along_core

    first_x, first_core = gather_rest(slice(0, 8))
    later_x, later_core = gather_rest(slice(8, 24))
    c_ring, cx, ccore, rz = {}, {}, {}, {}
    for h in thirds:
        third = lanes[h]

        def c_landed(o, third=third):
            source_far, source = ring_source(o)
            rows = pl.ds(at8(core * 128 + x * 32 + source * 8), 8)
            return c_all.at[source_far, rows, third]

        c_ring[h] = exchange(
            "ring",
            lambda o, third=third: c_all.at[far, pl.ds(base, 8), third],
            lambda o, third=third: c_all.at[far, pl.ds(base, 8), third],
            c_landed,
        )
        cx[h] = exchange(
            "x",
            lambda o, third=third: c_all.at[:, pl.ds(row32(0), 32), third],
            lambda o, third=third: c_all.at[:, pl.ds(row32(0), 32), third],
            lambda o, third=third: c_all.at[:, pl.ds(row32(o), 32), third],
        )
        ccore[h] = exchange(
            "core",
            lambda o, third=third: c_all.at[:, pl.ds(at8(core * 128, 128), 128), third],
            lambda o, third=third: c_all.at[:, pl.ds(at8(core * 128, 128), 128), third],
            lambda o, third=third: c_all.at[:, pl.ds(at8((1 - core) * 128, 128), 128), third],
        )
        rz[h] = exchange(
            "z",
            lambda o, third=third: right.at[pl.ds(at8(lax.rem(z + o, 8) * 32, 32), 32), third],
            lambda o, third=third: from_z.at[o - 1, :, third],
            lambda o, third=third: from_z.at[o - 1, :, third],
        )

    def c_to_ring(h):
        stage[h, "y"][1]()
        c_all[far, pl.ds(base, 8), lanes[h]] = add_y(lanes[h])
        c_ring[h][0]()

    def c_gather_x(h):
        c_ring[h][1]()
        cx[h][0]()

    def c_gather_core(h):
        cx[h][1]()
        ccore[h][0]()

    gz[0]()
    for h in thirds:
        c_to_y(h)
    gz[1]()
    ring_start()
    for h in thirds:
        c_to_ring(h)
    ring_wait(True)
    first_x[0]()
    c_gather_x(0)
    ring_wait(False)
    later_x[0]()
    first_x[1]()
    first_core[0]()
    c_gather_x(1)
    c_gather_x(2)
    w_all[pl.ds(at8(z * 32, 32), 32), :] = weight[:, pl.ds(at8(z * 512, 512), 512)]
    ring_sent()
    first_core[1]()

    total = jnp.zeros((8, TILE), F32)
    for s in range(16):
        total = total + g_all[s // 2, s % 2, FIRST // 4, FIRST % 4, 0:8, :]
    total = jnp.sum(jnp.sum(total, axis=0, keepdims=True), axis=1, keepdims=True)
    damping = 0.01 * total / 4096.0

    def place(i, j, unit_at):
        rows, cols = slice(i * TILE, (i + 1) * TILE), slice(j * TILE, (j + 1) * TILE)
        for e in range(16):
            m[i * TILE + 8 * e : i * TILE + 8 * e + 8, cols] = unit_at(e)
        block = m[rows, cols]
        if i == j:
            eye = lax.broadcasted_iota(jnp.int32, (TILE, TILE), 0) == lax.broadcasted_iota(
                jnp.int32, (TILE, TILE), 1
            )
            m[rows, cols] = block + jnp.where(eye, damping, 0.0)
        else:
            m[cols, rows] = block.T

    for i in range(NBLOCK):

        def first_unit(e, i=i):
            s, u = divmod(i * 16 + e, FIRST)
            return g_all[s // 2, s % 2, u // 4, u % 4, 0:8, :]

        place(i, 0, first_unit)

    def later_blocks():
        c_gather_core(0)
        later_x[1]()
        later_core[0]()
        c_gather_core(1)
        later_core[1]()
        block = 0
        for i in range(1, NBLOCK):
            for j in range(1, i + 1):

                def later_unit(e, block=block):
                    s, u = divmod(block * 16 + e, LATER)
                    q = u % 8
                    at = 8 * (1 + u // 8)
                    return g_all[s // 2, s % 2, q // 4, q % 4, at : at + 8, :]

                place(i, j, later_unit)
                block += 1

    def right_side(h):
        ccore[h][1]()
        for b in range(2):
            high, middle, low = pieces(c_all[b, :, lanes[h]])
            w = w_all[:, b * 256 : (b + 1) * 256]
            term = jnp.dot(w, high, preferred_element_type=F32)
            term += jnp.dot(w, middle, preferred_element_type=F32)
            term += jnp.dot(w, low, preferred_element_type=F32)
            if b == 0:
                right[:, lanes[h]] = term
            else:
                right[:, lanes[h]] += term
        rz[h][0]()

    @pl.loop(0, NBLOCK)
    def _(k):
        @pl.when(k == 1)
        def _():
            w_wait()
            right_side(0)
            c_gather_core(2)

        @pl.when(k == 2)
        def _():
            right_side(2)

        def arrive():
            @pl.when(k == 0)
            def _():
                later_blocks()

            @pl.when(k == 1)
            def _():
                right_side(1)

        eliminate(k, m, lower, n_tile, t_tile, scratch, left_pieces, right_pieces, arrive)

    for b in range(NBLOCK):
        rows = slice(b * TILE, (b + 1) * TILE)
        for i, p in enumerate(pieces(lower[rows, :])):
            lower_pieces[i, rows, :] = p
        for i, p in enumerate(pieces(m[rows, :])):
            m_pieces[i, rows, :] = p

    def times(v, factor, contract):
        stack = jnp.concatenate(pieces(v), axis=0)
        total = None
        for i in range(3):
            p = lax.dot_general(
                stack[0 : 32 * (3 - i), :], factor[i], (((1,), (contract,)), ((), ())),
                preferred_element_type=F32,
            )
            for at in range(3 - i):
                part_of = p[32 * at : 32 * at + 32, :]
                total = part_of if total is None else total + part_of
        return total

    for h in thirds:
        rz[h][1]()
    own = right[pl.ds(at8(z * 32, 32), 32), :]
    for o in range(7):
        own = own + from_z[o]
    out[...] = times(times(own, lower_pieces, 1), m_pieces, 0)


def spread_kernel(flags, solved, out):
    low = lax.broadcasted_iota(jnp.int32, (32, TILE), 1) < 64
    rank = jnp.int32(0)
    for g in range(32):
        sides = []
        for side in range(2):
            flag = flags[2 * g + side]
            at = jnp.minimum(rank, KEEP_BLK - 1)
            v = solved[:, pl.ds(pl.multiple_of((at // 2) * TILE, TILE), TILE)]
            v = jnp.where(at % 2 == side, v, _half_swap(v))
            sides.append(jnp.where(flag == 1, v, 0.0))
            rank = rank + flag
        out[:, g * TILE : (g + 1) * TILE] = jnp.where(low, sides[0], sides[1]).astype(BF16)


def on_device(tokens, orig_weight, keep_flags):
    vmem = pl.BlockSpec(memory_space=pltpu.VMEM)
    smem = pl.BlockSpec(memory_space=pltpu.SMEM)
    part = pl.pallas_call(
        prepare_kernel,
        out_shape=jax.ShapeDtypeStruct((256, WIDE), F32),
        in_specs=[smem, vmem],
        out_specs=vmem,
        scratch_shapes=[
            pltpu.SMEM((16,), jnp.int32),
            pltpu.VMEM((256, KEEP), BF16),
            pltpu.VMEM((KEEP, KEEP), F32),
        ],
        name="prepare",
    )(keep_flags, tokens)
    solved = pl.pallas_call(
        solve_kernel,
        out_shape=jax.ShapeDtypeStruct((32, KEEP), F32),
        in_specs=[vmem, vmem],
        out_specs=vmem,
        scratch_shapes=[
            pltpu.VMEM((128, WIDE), F32),
            pltpu.VMEM((3, 32, WIDE), F32),
            pltpu.VMEM((3, 8, WIDE), F32),
            pltpu.VMEM((128, WIDE), F32),
            pltpu.VMEM((32, WIDE), F32),
            pltpu.VMEM((8, 2, 2, 4, 32, TILE), F32),
            pltpu.VMEM((2, 256, KEEP), F32),
            pltpu.VMEM((256, 512), BF16),
            pltpu.VMEM((256, KEEP), F32),
            pltpu.VMEM((7, 32, KEEP), F32),
            pltpu.VMEM((KEEP, KEEP), F32),
            pltpu.VMEM((KEEP, KEEP), F32),
            pltpu.VMEM((TILE, TILE), F32),
            pltpu.VMEM((TILE, TILE), F32),
            pltpu.VMEM((8 * PANEL, TILE), F32),
            pltpu.VMEM((KEEP, KEEP), BF16),
            pltpu.VMEM((KEEP, KEEP), BF16),
            pltpu.VMEM((3, KEEP, KEEP), BF16),
            pltpu.VMEM((3, KEEP, KEEP), BF16),
            pltpu.SemaphoreType.DMA((128,)),
            pltpu.SemaphoreType.DMA((128,)),
        ],
        compiler_params=pltpu.CompilerParams(collective_id=0, has_side_effects=True),
        name="solve",
    )(part, orig_weight)
    return pl.pallas_call(
        spread_kernel,
        out_shape=jax.ShapeDtypeStruct((32, orig_weight.shape[1]), BF16),
        in_specs=[smem, vmem],
        out_specs=vmem,
        name="spread",
    )(keep_flags, solved)


def solution(mesh):
    in_specs = (P("dp", None), P(("section", "dp"), None), P())
    out_specs = P(("section", "dp"), None)
    return jax.shard_map(
        on_device, mesh=mesh, in_specs=in_specs, out_specs=out_specs, check_vma=False
    )
```

```python
import functools

import jax
import jax.numpy as jnp
from jax import lax
from jax.experimental import pallas as pl
from jax.experimental.pallas import tpu as pltpu
from jax.sharding import PartitionSpec as P

HIGHEST = lax.Precision.HIGHEST
F32 = jnp.float32
BF16 = jnp.bfloat16
MESH = pl.DeviceIdType.MESH

KEEP_BLK = 12
KEEP = 768
TILE = 128
PANEL = 8
NBLOCK = KEEP // TILE
FIRST = NBLOCK
LATER = NBLOCK * (NBLOCK - 1) // 2
WIDE = KEEP + TILE
CHUNK = 256


def _lower_block(t):
    row = jnp.int32(0)
    for i in range(1, NBLOCK - 1):
        row = row + (t >= i * (i + 1) // 2).astype(jnp.int32)
    return row, t - row * (row + 1) // 2


def _half_swap(v):
    return pltpu.roll(v, 64, 1)


def prepare_kernel(flags, tokens, part, kept, kept_tokens, gram):
    section = lax.axis_index("section")

    count = jnp.int32(0)
    for b in range(64):
        kept[count] = b
        count = count + flags[b]
    low = lax.broadcasted_iota(jnp.int32, (256, TILE), 1) < 64
    for i in range(NBLOCK):
        first, second = kept[2 * i], kept[2 * i + 1]
        a = tokens[:, pl.ds(pl.multiple_of((first // 2) * TILE, TILE), TILE)].astype(F32)
        b = tokens[:, pl.ds(pl.multiple_of((second // 2) * TILE, TILE), TILE)].astype(F32)
        a = jnp.where(first % 2 == 1, _half_swap(a), a)
        b = jnp.where(second % 2 == 0, _half_swap(b), b)
        kept_tokens[:, i * TILE : (i + 1) * TILE] = jnp.where(low, a, b).astype(BF16)
    chunk = tokens[:, pl.ds(pl.multiple_of(section * CHUNK, CHUNK), CHUNK)]
    over_tokens = (((0,), (0,)), ((), ()))
    part[:, 0:KEEP] = lax.dot_general(
        chunk, kept_tokens[...], over_tokens, preferred_element_type=F32
    )
    gram[...] = lax.dot_general(
        kept_tokens[...], kept_tokens[...], over_tokens, preferred_element_type=F32
    )
    part[:, KEEP:WIDE] = jnp.zeros((256, TILE), F32)

    def put(at, unit, row, col):
        start = row * TILE + (unit % 16) * 8
        part[at : at + 8, KEEP:WIDE] = gram[
            pl.ds(pl.multiple_of(start, 8), 8), pl.ds(pl.multiple_of(col * TILE, TILE), TILE)
        ]

    for u in range(FIRST):
        unit = section * FIRST + u
        put(32 * u, unit, unit // 16, 0)
    for u in range(LATER):
        unit = section * LATER + u
        row, col = _lower_block(unit // 16)
        put(32 * (u % 8) + 8 * (1 + u // 8), unit, row + 1, col + 1)
    wide = chunk.astype(F32)
    squares = wide * wide
    squares = squares[:, :TILE] + squares[:, TILE:]
    total = squares[0:8]
    for g in range(1, 32):
        total = total + squares[8 * g : 8 * g + 8]
    part[32 * FIRST : 32 * FIRST + 8, KEEP:WIDE] = total


def tile_factors(rows, n, t, scratch):
    lane = lax.broadcasted_iota(jnp.int32, (8, TILE), 1)
    sub = lax.broadcasted_iota(jnp.int32, (8, TILE), 0)
    panels = TILE // PANEL
    rows = list(rows)

    def over_lanes(v, c):
        column = jnp.sum(jnp.where(lane == c, v, 0.0), axis=1, keepdims=True)
        return jnp.broadcast_to(column, (8, TILE))

    def over_rows(v, q):
        return jnp.broadcast_to(v[q : q + 1, :], (8, TILE))

    for c in range(PANEL):
        scratch[8 * c : 8 * c + 8, :] = over_lanes(rows[0], c)
    columns = [scratch[8 * c : 8 * c + 8, :] for c in range(PANEL)]
    for j in range(panels):
        base = j * PANEL
        more = j + 1 < panels
        if more:
            ahead = [over_lanes(rows[j], base + PANEL + c) for c in range(PANEL)]
            below = [over_lanes(rows[j + 1], base + c) for c in range(PANEL)]
            coming = [over_lanes(rows[j + 1], base + PANEL + c) for c in range(PANEL)]
        inside = (lane >= base) & (lane < base + PANEL)
        r = jnp.where(inside, (lane - base == sub).astype(F32), rows[j])
        n[base : base + 8, :] = jnp.where(lane < base + PANEL, r, 0.0)
        for q in range(PANEL):
            inv = 1.0 / over_rows(columns[q], q)
            pivot = sub == q
            m = jnp.where(pivot, 0.0, columns[q] * inv)
            scale = jnp.where(pivot, inv, 1.0)
            r = r * scale - m * over_rows(r, q)
            for c in range(q + 1, PANEL):
                columns[c] = columns[c] * scale - m * over_rows(columns[c], q)
            if more:
                for c in range(PANEL):
                    ahead[c] = ahead[c] * scale - m * over_rows(ahead[c], q)
        t[base : base + 8, :] = jnp.where(lane < base + PANEL, r, 0.0)
        if more:
            columns = []
            for c in range(PANEL):
                terms = [below[q] * over_rows(ahead[c], q) for q in range(PANEL)]
                while len(terms) > 1:
                    terms = [a + b for a, b in zip(terms[::2], terms[1::2])]
                columns.append(coming[c] - terms[0])
        spread = [over_rows(r, c) for c in range(PANEL)]
        for g in range(j + 1, panels):
            acc = jnp.where(inside, 0.0, rows[g])
            for c in range(PANEL):
                factor = below[c] if g == j + 1 else over_lanes(rows[g], base + c)
                acc = acc - factor * spread[c]
            rows[g] = acc


def pieces(v):
    high = v.astype(BF16)
    v = v - high.astype(F32)
    middle = v.astype(BF16)
    return high, middle, (v - middle.astype(F32)).astype(BF16)


def put_left(ref, rows, v):
    high, middle, low = pieces(v)
    for i, p in enumerate((high, high, middle, middle, high, low)):
        ref[rows, i * TILE : (i + 1) * TILE] = p


def put_right(ref, v):
    high, middle, low = pieces(v)
    for i, p in enumerate((high, middle, high, middle, low, high)):
        ref[i * TILE : (i + 1) * TILE, :] = p


def eliminate(k, m, lower, n, t, scratch, left, right, arrive):
    off = pl.multiple_of(k * TILE, TILE)
    rows = [m[pl.ds(pl.multiple_of(off + 8 * g, 8), 8), pl.ds(off, TILE)] for g in range(TILE // 8)]
    tile_factors(rows, n, t, scratch)
    arrive()
    d = lax.dot_general(
        n[...], t[...], (((0,), (0,)), ((), ())), precision=HIGHEST, preferred_element_type=F32
    )
    col = lax.broadcasted_iota(jnp.int32, (TILE, KEEP), 1) - off
    row = lax.broadcasted_iota(jnp.int32, (TILE, KEEP), 0)
    inside = (col >= 0) & (col < TILE)
    r = jnp.where(inside, (col == row).astype(F32), m[pl.ds(off, TILE), :])
    lower[pl.ds(off, TILE), :] = jnp.where(col < TILE, r, 0.0)
    put_left(left, slice(0, TILE), d)
    put_right(right, r)
    r = jnp.dot(left[0:TILE, :], right[...], preferred_element_type=F32)
    m[pl.ds(off, TILE), :] = jnp.where(col < TILE, r, 0.0)
    put_right(right, r)
    for kk in range(NBLOCK - 1):

        @pl.when(k == kk)
        def _():
            start = kk * TILE
            stop = start + TILE
            put_left(left, slice(stop, KEEP), m[stop:KEEP, start:stop])
            p = jnp.dot(left[stop:KEEP, :], right[...], preferred_element_type=F32)
            if kk:
                m[stop:KEEP, 0:start] = m[stop:KEEP, 0:start] - p[:, 0:start]
            m[stop:KEEP, start:stop] = -p[:, start:stop]
            m[stop:KEEP, stop:KEEP] = m[stop:KEEP, stop:KEEP] - p[:, stop:KEEP]


def solve_kernel(
    part, weight, out,
    from_core, from_x, from_y, sums, shares, g_all, c_all, w_all, right, from_z,
    m, lower, n_tile, t_tile, scratch, left_pieces, right_pieces, lower_pieces, m_pieces, send, recv,
):
    section, dp = lax.axis_index("section"), lax.axis_index("dp")
    z, far = section // 2, section % 2
    x, y, core = dp // 8, (dp // 2) % 4, dp % 2
    slot = lax.rem(y + 3, 4)

    def peer(axis, o):
        if axis == "z":
            return (lax.rem(z + o, 8) * 2 + far, dp)
        if axis == "ring":
            at = lax.rem(far * 4 + y + o, 8)
            return (z * 2 + at // 4, x * 8 + lax.rem(at, 4) * 2 + core)
        if axis == "x":
            return (section, lax.rem(x + o, 4) * 8 + y * 2 + core)
        if axis == "y":
            return (section, x * 8 + lax.rem(y + o, 4) * 2 + core)
        return (section, x * 8 + y * 2 + 1 - core)

    sizes = {"z": 8, "ring": 8, "x": 4, "y": 4, "core": 2}
    barrier = pltpu.get_barrier_semaphore()
    greeted = 0
    for axis in ("z", "ring", "x", "core"):
        for o in range(1, sizes[axis]):
            pl.semaphore_signal(barrier, inc=1, device_id=peer(axis, o), device_id_type=MESH)
            greeted += 1
    pl.semaphore_wait(barrier, greeted)

    slots = [0]
    all_sent = []

    def exchange(axis, source, target, landed):
        first = slots[0]
        n = sizes[axis]
        slots[0] += n - 1

        def copy(o, dst):
            at = first + o - 1
            return pltpu.make_async_remote_copy(
                src_ref=source(o), dst_ref=dst, send_sem=send.at[at], recv_sem=recv.at[at],
                device_id=peer(axis, o), device_id_type=MESH,
            )

        def start():
            for o in range(1, n):
                copy(o, target(o)).start()

        def wait():
            for o in range(1, n):
                copy(o, landed(o)).wait_recv()

        def sent():
            for o in range(1, n):
                copy(o, target(o)).wait_send()

        all_sent.append(sent)
        return start, wait

    def at8(v, n=8):
        return pl.multiple_of(v, n)

    w_start, w_wait = exchange(
        "z",
        lambda o: weight.at[:, pl.ds(at8(lax.rem(z + o, 8) * 512, 512), 512)],
        lambda o: w_all.at[pl.ds(at8(z * 32, 32), 32), :],
        lambda o: w_all.at[pl.ds(at8(lax.rem(z + 8 - o, 8) * 32, 32), 32), :],
    )
    w_start()

    thirds = (0, 1, 2)
    lanes = {"g": slice(KEEP, WIDE)}
    for h in thirds:
        lanes[h] = slice(h * KEEP // 3, (h + 1) * KEEP // 3)
    stage = {}
    for name in ("g", *thirds):
        cut = lanes[name]
        stage[name, "core"] = exchange(
            "core",
            lambda o, cut=cut: part.at[pl.ds(at8((1 - core) * 128, 128), 128), cut],
            lambda o, cut=cut: from_core.at[:, cut],
            lambda o, cut=cut: from_core.at[:, cut],
        )
        stage[name, "x"] = exchange(
            "x",
            lambda o, cut=cut: sums.at[pl.ds(at8(lax.rem(x + o, 4) * 32, 32), 32), cut],
            lambda o, cut=cut: from_x.at[o - 1, :, cut],
            lambda o, cut=cut: from_x.at[o - 1, :, cut],
        )
        stage[name, "y"] = exchange(
            "y",
            lambda o, cut=cut: shares.at[pl.ds(at8(lax.rem(slot + o, 4) * 8), 8), cut],
            lambda o, cut=cut: from_y.at[o - 1, :, cut],
            lambda o, cut=cut: from_y.at[o - 1, :, cut],
        )

    def add_core(cut):
        sums[:, cut] = part[pl.ds(at8(core * 128, 128), 128), cut] + from_core[:, cut]

    def add_x(cut):
        own = sums[pl.ds(at8(x * 32, 32), 32), cut]
        shares[:, cut] = own + from_x[0, :, cut] + from_x[1, :, cut] + from_x[2, :, cut]

    def add_y(cut):
        own = shares[pl.ds(at8(slot * 8), 8), cut]
        return own + from_y[0, :, cut] + from_y[1, :, cut] + from_y[2, :, cut]

    base = at8(core * 128 + x * 32 + slot * 8)
    g_cut = lanes["g"]
    stage["g", "core"][0]()
    for h in thirds:
        stage[h, "core"][0]()

    def c_to_x(h):
        stage[h, "core"][1]()
        add_core(lanes[h])
        stage[h, "x"][0]()

    def c_to_y(h):
        stage[h, "x"][1]()
        add_x(lanes[h])
        stage[h, "y"][0]()

    stage["g", "core"][1]()
    add_core(g_cut)
    stage["g", "x"][0]()
    c_to_x(0)
    stage["g", "x"][1]()
    add_x(g_cut)
    stage["g", "y"][0]()
    c_to_x(1)
    c_to_x(2)
    stage["g", "y"][1]()
    own8 = pl.ds(at8(slot * 8), 8)
    g_all[z, far, core, x, own8, :] = add_y(g_cut)

    gz = exchange(
        "z",
        lambda o: g_all.at[z, far, core, x, own8, :],
        lambda o: g_all.at[z, far, core, x, own8, :],
        lambda o: g_all.at[lax.rem(z + 8 - o, 8), far, core, x, own8, :],
    )
    def ring_source(o):
        at = lax.rem(far * 4 + y + 8 - o, 8)
        return at // 4, lax.rem(at + 3, 4)

    def row32(o):
        return at8(core * 128 + lax.rem(x + 4 - o, 4) * 32, 32)

    ring_slots = slots[0]
    slots[0] += 7

    def ring_copy(o, dst):
        at = ring_slots + o - 1
        return pltpu.make_async_remote_copy(
            src_ref=g_all.at[:, far, core, x, own8, :], dst_ref=dst, send_sem=send.at[at],
            recv_sem=recv.at[at], device_id=peer("ring", o), device_id_type=MESH,
        )

    def ring_start():
        @pl.when(slot < 3)
        def _():
            for o in range(1, 8):
                ring_copy(o, g_all.at[:, far, core, x, own8, :]).start()

    def ring_sent():
        @pl.when(slot < 3)
        def _():
            for o in range(1, 8):
                ring_copy(o, g_all.at[:, far, core, x, own8, :]).wait_send()

    def ring_wait(first):
        for o in range(1, 8):
            source_far, source = ring_source(o)

            @pl.when((source == 0) if first else ((source == 1) | (source == 2)))
            def _():
                rows = pl.ds(at8(source * 8), 8)
                ring_copy(o, g_all.at[:, source_far, core, x, rows, :]).wait_recv()

    def gather_rest(rows):
        along_x = exchange(
            "x",
            lambda o: g_all.at[:, :, core, x, rows, :],
            lambda o: g_all.at[:, :, core, x, rows, :],
            lambda o: g_all.at[:, :, core, lax.rem(x + 4 - o, 4), rows, :],
        )
        along_core = exchange(
            "core",
            lambda o: g_all.at[:, :, core, :, rows, :],
            lambda o: g_all.at[:, :, core, :, rows, :],
            lambda o: g_all.at[:, :, 1 - core, :, rows, :],
        )
        return along_x, along_core

    first_x, first_core = gather_rest(slice(0, 8))
    later_x, later_core = gather_rest(slice(8, 24))
    c_ring, cx, ccore, rz = {}, {}, {}, {}
    for h in thirds:
        third = lanes[h]

        def c_landed(o, third=third):
            source_far, source = ring_source(o)
            rows = pl.ds(at8(core * 128 + x * 32 + source * 8), 8)
            return c_all.at[source_far, rows, third]

        c_ring[h] = exchange(
            "ring",
            lambda o, third=third: c_all.at[far, pl.ds(base, 8), third],
            lambda o, third=third: c_all.at[far, pl.ds(base, 8), third],
            c_landed,
        )
        cx[h] = exchange(
            "x",
            lambda o, third=third: c_all.at[:, pl.ds(row32(0), 32), third],
            lambda o, third=third: c_all.at[:, pl.ds(row32(0), 32), third],
            lambda o, third=third: c_all.at[:, pl.ds(row32(o), 32), third],
        )
        ccore[h] = exchange(
            "core",
            lambda o, third=third: c_all.at[:, pl.ds(at8(core * 128, 128), 128), third],
            lambda o, third=third: c_all.at[:, pl.ds(at8(core * 128, 128), 128), third],
            lambda o, third=third: c_all.at[:, pl.ds(at8((1 - core) * 128, 128), 128), third],
        )
        rz[h] = exchange(
            "z",
            lambda o, third=third: right.at[pl.ds(at8(lax.rem(z + o, 8) * 32, 32), 32), third],
            lambda o, third=third: from_z.at[o - 1, :, third],
            lambda o, third=third: from_z.at[o - 1, :, third],
        )

    def c_to_ring(h):
        stage[h, "y"][1]()
        c_all[far, pl.ds(base, 8), lanes[h]] = add_y(lanes[h])
        c_ring[h][0]()

    def c_gather_x(h):
        c_ring[h][1]()
        cx[h][0]()

    def c_gather_core(h):
        cx[h][1]()
        ccore[h][0]()

    gz[0]()
    for h in thirds:
        c_to_y(h)
    gz[1]()
    ring_start()
    for h in thirds:
        c_to_ring(h)
    ring_wait(True)
    first_x[0]()
    c_gather_x(0)
    ring_wait(False)
    later_x[0]()
    first_x[1]()
    first_core[0]()
    c_gather_x(1)
    c_gather_x(2)
    w_all[pl.ds(at8(z * 32, 32), 32), :] = weight[:, pl.ds(at8(z * 512, 512), 512)]
    all_sent.append(ring_sent)
    first_core[1]()

    total = jnp.zeros((8, TILE), F32)
    for s in range(16):
        total = total + g_all[s // 2, s % 2, FIRST // 4, FIRST % 4, 0:8, :]
    total = jnp.sum(jnp.sum(total, axis=0, keepdims=True), axis=1, keepdims=True)
    damping = 0.01 * total / 4096.0

    def place(i, j, unit_at):
        rows, cols = slice(i * TILE, (i + 1) * TILE), slice(j * TILE, (j + 1) * TILE)
        for e in range(16):
            m[i * TILE + 8 * e : i * TILE + 8 * e + 8, cols] = unit_at(e)
        block = m[rows, cols]
        if i == j:
            eye = lax.broadcasted_iota(jnp.int32, (TILE, TILE), 0) == lax.broadcasted_iota(
                jnp.int32, (TILE, TILE), 1
            )
            m[rows, cols] = block + jnp.where(eye, damping, 0.0)
        else:
            m[cols, rows] = block.T

    for i in range(NBLOCK):

        def first_unit(e, i=i):
            s, u = divmod(i * 16 + e, FIRST)
            return g_all[s // 2, s % 2, u // 4, u % 4, 0:8, :]

        place(i, 0, first_unit)

    def later_blocks():
        c_gather_core(0)
        later_x[1]()
        later_core[0]()
        c_gather_core(1)
        later_core[1]()
        block = 0
        for i in range(1, NBLOCK):
            for j in range(1, i + 1):

                def later_unit(e, block=block):
                    s, u = divmod(block * 16 + e, LATER)
                    q = u % 8
                    at = 8 * (1 + u // 8)
                    return g_all[s // 2, s % 2, q // 4, q % 4, at : at + 8, :]

                place(i, j, later_unit)
                block += 1

    def right_side(h):
        ccore[h][1]()
        for b in range(2):
            high, middle, low = pieces(c_all[b, :, lanes[h]])
            w = w_all[:, b * 256 : (b + 1) * 256]
            term = jnp.dot(w, high, preferred_element_type=F32)
            term += jnp.dot(w, middle, preferred_element_type=F32)
            term += jnp.dot(w, low, preferred_element_type=F32)
            if b == 0:
                right[:, lanes[h]] = term
            else:
                right[:, lanes[h]] += term
        rz[h][0]()

    @pl.loop(0, NBLOCK)
    def _(k):
        @pl.when(k == 1)
        def _():
            w_wait()
            right_side(0)
            c_gather_core(2)

        @pl.when(k == 2)
        def _():
            right_side(2)

        def arrive():
            @pl.when(k == 0)
            def _():
                later_blocks()

            @pl.when(k == 1)
            def _():
                right_side(1)

        eliminate(k, m, lower, n_tile, t_tile, scratch, left_pieces, right_pieces, arrive)

    for b in range(NBLOCK):
        rows = slice(b * TILE, (b + 1) * TILE)
        for i, p in enumerate(pieces(lower[rows, :])):
            lower_pieces[i, rows, :] = p
        for i, p in enumerate(pieces(m[rows, :])):
            m_pieces[i, rows, :] = p

    def times(v, factor, contract):
        stack = jnp.concatenate(pieces(v), axis=0)
        total = None
        for i in range(3):
            p = lax.dot_general(
                stack[0 : 32 * (3 - i), :], factor[i], (((1,), (contract,)), ((), ())),
                preferred_element_type=F32,
            )
            for at in range(3 - i):
                part_of = p[32 * at : 32 * at + 32, :]
                total = part_of if total is None else total + part_of
        return total

    for h in thirds:
        rz[h][1]()
    own = right[pl.ds(at8(z * 32, 32), 32), :]
    for o in range(7):
        own = own + from_z[o]
    out[...] = times(times(own, lower_pieces, 1), m_pieces, 0)
    for sent in all_sent:
        sent()


def spread_kernel(flags, solved, out):
    low = lax.broadcasted_iota(jnp.int32, (32, TILE), 1) < 64
    rank = jnp.int32(0)
    for g in range(32):
        sides = []
        for side in range(2):
            flag = flags[2 * g + side]
            at = jnp.minimum(rank, KEEP_BLK - 1)
            v = solved[:, pl.ds(pl.multiple_of((at // 2) * TILE, TILE), TILE)]
            v = jnp.where(at % 2 == side, v, _half_swap(v))
            sides.append(jnp.where(flag == 1, v, 0.0))
            rank = rank + flag
        out[:, g * TILE : (g + 1) * TILE] = jnp.where(low, sides[0], sides[1]).astype(BF16)


def on_device(tokens, orig_weight, keep_flags):
    vmem = pl.BlockSpec(memory_space=pltpu.VMEM)
    smem = pl.BlockSpec(memory_space=pltpu.SMEM)
    part = pl.pallas_call(
        prepare_kernel,
        out_shape=jax.ShapeDtypeStruct((256, WIDE), F32),
        in_specs=[smem, vmem],
        out_specs=vmem,
        scratch_shapes=[
            pltpu.SMEM((16,), jnp.int32),
            pltpu.VMEM((256, KEEP), BF16),
            pltpu.VMEM((KEEP, KEEP), F32),
        ],
        name="prepare",
    )(keep_flags, tokens)
    solved = pl.pallas_call(
        solve_kernel,
        out_shape=jax.ShapeDtypeStruct((32, KEEP), F32),
        in_specs=[vmem, vmem],
        out_specs=vmem,
        scratch_shapes=[
            pltpu.VMEM((128, WIDE), F32),
            pltpu.VMEM((3, 32, WIDE), F32),
            pltpu.VMEM((3, 8, WIDE), F32),
            pltpu.VMEM((128, WIDE), F32),
            pltpu.VMEM((32, WIDE), F32),
            pltpu.VMEM((8, 2, 2, 4, 32, TILE), F32),
            pltpu.VMEM((2, 256, KEEP), F32),
            pltpu.VMEM((256, 512), BF16),
            pltpu.VMEM((256, KEEP), F32),
            pltpu.VMEM((7, 32, KEEP), F32),
            pltpu.VMEM((KEEP, KEEP), F32),
            pltpu.VMEM((KEEP, KEEP), F32),
            pltpu.VMEM((TILE, TILE), F32),
            pltpu.VMEM((TILE, TILE), F32),
            pltpu.VMEM((8 * PANEL, TILE), F32),
            pltpu.VMEM((KEEP, KEEP), BF16),
            pltpu.VMEM((KEEP, KEEP), BF16),
            pltpu.VMEM((3, KEEP, KEEP), BF16),
            pltpu.VMEM((3, KEEP, KEEP), BF16),
            pltpu.SemaphoreType.DMA((128,)),
            pltpu.SemaphoreType.DMA((128,)),
        ],
        compiler_params=pltpu.CompilerParams(collective_id=0, has_side_effects=True),
        name="solve",
    )(part, orig_weight)
    return pl.pallas_call(
        spread_kernel,
        out_shape=jax.ShapeDtypeStruct((32, orig_weight.shape[1]), BF16),
        in_specs=[smem, vmem],
        out_specs=vmem,
        name="spread",
    )(keep_flags, solved)


def solution(mesh):
    in_specs = (P("dp", None), P(("section", "dp"), None), P())
    out_specs = P(("section", "dp"), None)
    return jax.shard_map(
        on_device, mesh=mesh, in_specs=in_specs, out_specs=out_specs, check_vma=False
    )
```
